32 devices in a mesh: dp: 8 (over z, y), tensor: 4 (over x, core).
Axes of the slice: x: 2, y: 2, z: 4, core: 2. Of those that a mesh axis runs over, the one named last changes fastest.
Arguments:
- tokens: bfloat16 [4096, 2048], P('dp'), may hold values from -6 to 6
- seq_blocks: int32 [3], replicated, may hold values from 8 to 16, as said below
- block_place: int32 [32], replicated, may hold values from 0 to 31, as said below
- pad_mask: int32 [4096], P('dp'), may hold values from 0 to 1, as said below
- expert_ids: int32 [4096, 8], P('dp'), may hold values from 0 to 63, as said below
- attn_gain: float32 [2048], replicated, may hold values from 0.25 to 1.75
- w_qkv: bfloat16 [2048, 3, 2048], P(None, None, 'tensor'), may hold values from -0.125 to 0.125
- qk_gain: float32 [2, 2048], P(None, 'tensor'), may hold values from 0.25 to 1.75
- w_out: bfloat16 [2048, 2048], P('tensor'), may hold values from -1 to 1
- ffn_gain: float32 [2048], replicated, may hold values from 0.25 to 1.75
- router: bfloat16 [2048, 64], replicated, may hold values from -0.15625 to 0.15625
- expert_in: bfloat16 [2, 2048, 2, 1024], P(None, None, None, 'tensor'), may hold values from -0.125 to 0.125
- expert_out: bfloat16 [2, 1024, 2048], P(None, 'tensor'), may hold values from -16 to 16
- cotangent: bfloat16 [4096, 2048], P('dp', 'tensor'), may hold values from -6 to 6
Outputs:
- output: bfloat16 [4096, 2048], P('dp', 'tensor')
- input_grad: bfloat16 [4096, 2048], P('dp', 'tensor')
- grad_attn_gain: float32 [2048], P('tensor')
- grad_qkv: float32 [2048, 3, 2048], P(None, None, 'tensor')
- grad_qk_gain: float32 [2, 2048], P(None, 'tensor')
- grad_out: float32 [2048, 2048], P('tensor')
- grad_ffn_gain: float32 [2048], P('tensor')
- grad_router: float32 [2048, 64], P('tensor')
- grad_expert_in: float32 [2, 2048, 2, 1024], P(None, None, None, 'tensor')
- grad_expert_out: float32 [2, 1024, 2048], P(None, 'tensor')
The draws below stay inside these ranges and needn't reach their ends.
Inputs may be any that keep to these rules, and one draw needn't show every extreme that they name: `seq_blocks`: they sum to 32; each is at least 8; the largest is exactly 16. A permutation: rows b * 128 to (b + 1) * 128 - 1 of the given order are packed block block_place[b]. `pad_mask`: zeros only at the end of each sequence, in its last two packed blocks: from 128 to 255 of its last tokens. `expert_ids`: each row names 8 different experts; in the rows of one index of dp (aligned blocks of 512 rows) each expert below 2 is named by at most 128 rows, and by exactly 128 rows in some block.
All inputs are finite; a program needn't handle non-finite values.
Results may differ from the reference program's by a relative error of at most 0.029.
Values may be sent and summed in bfloat16 or wider, within the bound.
A program may use at most 384 MiB of HBM per device.

```python
import jax
import jax.numpy as jnp
from jax import lax

D = 2048
HEADS = 16
HDIM = 128
EXPERTS_ALL = 64
TOPK = 8
FFE = 1024
WIN = 2
TOK_DEV = 512
BLOCK = 128
TOKENS = 4096
NBLK = 32
NSEQ = 3
MINB = 8
MAXB = 16
CAP = 128


def layout_draw(key):
    base_key = jax.random.fold_in(key, 11)
    key_share, key_long, key_place, key_pads = jax.random.split(base_key, 4)
    spare = NBLK - MAXB - (NSEQ - 1) * MINB
    weights = jax.random.randint(key_share, (NSEQ - 1,), 2, 5)
    extra = spare * weights // jnp.maximum(jnp.sum(weights), 1)
    leftover = spare - jnp.sum(extra)
    extra = extra + (jnp.arange(NSEQ - 1) < leftover).astype(jnp.int32)
    values = jnp.concatenate([jnp.full((1,), MAXB, jnp.int32), (MINB + extra).astype(jnp.int32)])
    seq_blocks = jax.random.permutation(key_long, values).astype(jnp.int32)
    block_place = jax.random.permutation(key_place, NBLK).astype(jnp.int32)
    pad_counts = jax.random.randint(key_pads, (NSEQ,), BLOCK, 2 * BLOCK)
    row_ids = jnp.arange(TOKENS, dtype=jnp.int32)
    packed = block_place[row_ids // BLOCK]
    seq_ends = jnp.cumsum(seq_blocks).astype(jnp.int32)
    seq_of = jnp.sum((packed[:, None] >= seq_ends[None, :]).astype(jnp.int32), axis=1)
    from_end = (seq_ends[seq_of] - 1 - packed) * BLOCK + (BLOCK - 1 - row_ids % BLOCK)
    pad_mask = 1 - (from_end < pad_counts[seq_of]).astype(jnp.int32)
    return (seq_blocks, block_place, pad_mask.astype(jnp.int32))


def draw_seq_blocks(key, part):
    return layout_draw(key)[0]


def draw_block_place(key, part):
    return layout_draw(key)[1]


def draw_pad_mask(key, part):
    return layout_draw(key)[2]


def draw_expert_ids(key, part):
    base_key = jax.random.fold_in(key, 23)
    key_count, key_full, key_rank, key_rest = jax.random.split(base_key, 4)
    block_total = TOKENS // TOK_DEV
    counts = jax.random.randint(key_count, (block_total, WIN), CAP // 4, CAP + 1)
    full_at = jax.random.randint(key_full, (WIN,), 0, block_total)
    counts = jnp.where(jnp.arange(block_total)[:, None] == full_at[None, :], CAP, counts)
    rank_keys = jax.random.split(key_rank, block_total * WIN)
    rank_table = jax.vmap(lambda sub_key: jax.random.permutation(sub_key, TOK_DEV))(rank_keys).reshape(block_total, WIN, TOK_DEV)
    member = rank_table < counts[:, :, None]
    member = jnp.transpose(member, (0, 2, 1)).reshape(TOKENS, WIN)
    window = jnp.arange(WIN, dtype=jnp.int32)[None, :]
    inside = jnp.where(member, (1 << 28) + window, -1 - window)
    scores = jax.random.randint(key_rest, (TOKENS, EXPERTS_ALL - WIN), 0, 1 << 20) * EXPERTS_ALL + jnp.arange(WIN, EXPERTS_ALL, dtype=jnp.int32)[None, :]
    _, picked = lax.top_k(jnp.concatenate([inside, scores.astype(jnp.int32)], axis=1), TOPK)
    return picked.astype(jnp.int32)


def shard_levels(key, extent, cuts, least, high):
    factor_of, own = 1.0, jax.random.fold_in(key, 6)
    for axis_at, shards_of in cuts:
        draws = jnp.exp(jax.random.uniform(jax.random.fold_in(own, axis_at), (shards_of,), jnp.float32, least / len(cuts), high / len(cuts)))
        factor_of = factor_of * jnp.repeat(draws, extent[axis_at] // shards_of).reshape([-1 if axis == axis_at else 1 for axis in range(len(extent))])
    return factor_of


def normal_values(key, shape, deviation, reach, cuts=(), kind=jnp.bfloat16):
    result = deviation * jax.random.normal(key, shape, jnp.float32)
    if cuts:
        result = result * shard_levels(key, shape, cuts, -0.22, 0.18)
    return jnp.clip(result, -reach, reach).astype(kind)


def setup_inputs(seed: int = 0) -> dict:
    streams_of = jax.random.split(jax.random.key(seed), 15)
    return {
        "tokens": normal_values(streams_of[0], (TOKENS, D), 1.0, 6.0, ((0, 8),)),
        "seq_blocks": draw_seq_blocks(jax.random.fold_in(streams_of[14], 71), 0),
        "block_place": draw_block_place(jax.random.fold_in(streams_of[14], 71), 0),
        "pad_mask": draw_pad_mask(jax.random.fold_in(streams_of[14], 71), 0),
        "expert_ids": draw_expert_ids(jax.random.fold_in(streams_of[14], 71), 0),
        "attn_gain": jnp.clip(1.0 + 0.15 * jax.random.normal(streams_of[5], (D,), jnp.float32), 0.25, 1.75),
        "w_qkv": normal_values(streams_of[6], (D, 3, D), D ** -0.5, 0.125, ((2, 4),)),
        "qk_gain": jnp.clip(1.0 + 0.15 * jax.random.normal(streams_of[7], (2, D), jnp.float32), 0.25, 1.75),
        "w_out": normal_values(streams_of[8], (D, D), (max(1, D // 64)) ** -0.5, 1.0, ((0, 4),)),
        "ffn_gain": jnp.clip(1.0 + 0.15 * jax.random.normal(streams_of[9], (D,), jnp.float32), 0.25, 1.75),
        "router": normal_values(streams_of[10], (D, EXPERTS_ALL), (0.5 / D ** 0.5), 0.15625),
        "expert_in": normal_values(streams_of[11], (WIN, D, 2, FFE), D ** -0.5, 0.125, ((3, 4),)),
        "expert_out": normal_values(streams_of[12], (WIN, FFE, D), (1.5 * EXPERTS_ALL / FFE ** 0.5), 16.0, ((1, 4),)),
        "cotangent": normal_values(streams_of[13], (TOKENS, D), 1.0, 6.0, ((0, 8), (1, 4))),
    }


EPSILON = 1e-05
ROPE_BASE = 10000.0
NEGATIVE = -1e+30

@jax.custom_vjp
def low(v):
    return lax.optimization_barrier(v.astype(jnp.bfloat16)).astype(jnp.float32)

@jax.custom_vjp
def low_back(v):
    return v

def low_keep(v):
    return (low(v), None)

def low_pass(kept, grad):
    return (grad,)

def back_keep(v):
    return (v, None)

def back_low(kept, grad):
    return (low(grad),)
low.defvjp(low_keep, low_pass)
low_back.defvjp(back_keep, back_low)

def exact_dot(left, right):
    return jnp.dot(left, right, precision=lax.Precision.HIGHEST, preferred_element_type=jnp.float32)

def row_scale(values):
    return lax.rsqrt(lax.optimization_barrier(jnp.mean(values * values, axis=-1, keepdims=True)) + EPSILON)

def rotate(values, positions):
    half_dim = values.shape[-1] // 2
    inv_freq = ROPE_BASE ** (-(jnp.arange(half_dim, dtype=jnp.float32) * 2.0) / values.shape[-1])
    turn_angle = positions.astype(jnp.float32)[:, None] * inv_freq[None, :]
    cosine = jnp.cos(turn_angle)[:, None, :]
    sine_vals = jnp.sin(turn_angle)[:, None, :]
    first_half = values[..., :half_dim]
    second_half = values[..., half_dim:]
    return jnp.concatenate([first_half * cosine - second_half * sine_vals, second_half * cosine + first_half * sine_vals], axis=-1)

def token_tables(seq_blocks, block_place, row_ids):
    block_total = block_place.shape[0]
    seq_total = seq_blocks.shape[0]
    seq_ends = jnp.cumsum(seq_blocks).astype(jnp.int32)
    seq_firsts = seq_ends - seq_blocks
    given_block = row_ids // BLOCK
    packed = lax.optimization_barrier(jnp.sum(jnp.where(given_block[:, None] == jnp.arange(block_total, dtype=jnp.int32)[None, :], block_place[None, :], 0), axis=1))
    seq_of = lax.optimization_barrier(jnp.sum((packed[:, None] >= seq_ends[None, :]).astype(jnp.int32), axis=1))
    first_of = lax.optimization_barrier(jnp.sum(jnp.where(seq_of[:, None] == jnp.arange(seq_total, dtype=jnp.int32)[None, :], seq_firsts[None, :], 0), axis=1))
    return (seq_of, (packed - first_of) * BLOCK + row_ids % BLOCK)

def attend_block(query_rows, seg_rows, pos_rows, key_rows, value_rows, seg_cols, pos_cols, keep_cols):
    raw_scores = low_back(jnp.einsum('qhd,khd->hqk', query_rows, key_rows, precision=lax.Precision.HIGHEST))
    allowed = (seg_rows[:, None] == seg_cols[None, :]) & (pos_cols[None, :] <= pos_rows[:, None]) & (keep_cols[None, :] > 0)
    scores = jnp.where(allowed[None], raw_scores * HDIM ** (-0.5), NEGATIVE)
    row_top = lax.optimization_barrier(jnp.max(scores, axis=-1, keepdims=True))
    weights = jnp.exp(scores - row_top)
    row_total = lax.optimization_barrier(jnp.sum(weights, axis=-1))
    summed = low_back(jnp.einsum('hqk,khd->qhd', low(weights), value_rows, precision=lax.Precision.HIGHEST))
    return summed / jnp.transpose(row_total)[:, :, None]

def attention(q_turn, k_turn, value_heads, seq_ids, positions, keep_mask):
    query_block = min(512, TOKENS)
    block_count = TOKENS // query_block
    checked = jax.checkpoint(attend_block)

    def attend_rows(pieces):
        return checked(pieces[0], pieces[1], pieces[2], k_turn, value_heads, seq_ids, positions, keep_mask)
    result_rows = lax.map(attend_rows, (q_turn.reshape(block_count, query_block, HEADS, HDIM), seq_ids.reshape(block_count, query_block), positions.reshape(block_count, query_block)))
    return result_rows.reshape(TOKENS, HEADS, HDIM)

def reference(tokens, seq_blocks, block_place, pad_mask, expert_ids, attn_gain, w_qkv, qk_gain, w_out, ffn_gain, router, expert_in, expert_out, cotangent):
    row_ids = jnp.arange(TOKENS, dtype=jnp.int32)
    seq_ids, positions = token_tables(seq_blocks, block_place, row_ids)
    chosen = jnp.any(expert_ids[:, :, None] == jnp.arange(WIN, dtype=jnp.int32)[None, None, :], axis=1).astype(jnp.float32)

    def layer(inputs, g_attn, w_proj, g_qk, w_back, g_ffn, w_router, w_in, w_exp):
        normed_in = low(inputs * row_scale(inputs) * g_attn)
        projected = exact_dot(normed_in, w_proj.reshape(D, 3 * D)).reshape(TOKENS, 3, D)
        queries = low_back(projected[:, 0])
        keys_all = low_back(projected[:, 1])
        values_all = low_back(low(projected[:, 2]))
        q_turn = low(rotate((queries * row_scale(queries) * g_qk[0]).reshape(TOKENS, HEADS, HDIM), positions))
        k_turn = low(rotate((keys_all * row_scale(keys_all) * g_qk[1]).reshape(TOKENS, HEADS, HDIM), positions))
        attended = attention(q_turn, k_turn, values_all.reshape(TOKENS, HEADS, HDIM), seq_ids, positions, pad_mask)
        attended = low_back(low(attended))
        hidden = inputs + low_back(exact_dot(attended.reshape(TOKENS, D), w_back))
        normed = low(hidden * row_scale(hidden) * g_ffn)
        router_probs = jax.nn.softmax(low_back(exact_dot(normed, w_router)), axis=-1)
        mixture = jnp.zeros((TOKENS, D), jnp.float32)
        for expert in range(WIN):
            gate_up = exact_dot(normed, w_in[expert].reshape(D, 2 * FFE)).reshape(TOKENS, 2, FFE)
            active = low(jax.nn.silu(low_back(gate_up[:, 0])) * low_back(gate_up[:, 1]))
            expert_part = low_back(exact_dot(active, w_exp[expert]))
            mixture = mixture + (router_probs[:, expert] * chosen[:, expert])[:, None] * expert_part
        return hidden + mixture
    result_out, pullback = jax.vjp(layer, tokens.astype(jnp.float32), attn_gain, w_qkv.astype(jnp.float32), qk_gain, w_out.astype(jnp.float32), ffn_gain, router.astype(jnp.float32), expert_in.astype(jnp.float32), expert_out.astype(jnp.float32))
    gradients = pullback(cotangent.astype(jnp.float32))
    return (result_out.astype(jnp.bfloat16), gradients[0].astype(jnp.bfloat16), gradients[1], gradients[2], gradients[3], gradients[4], gradients[5], gradients[6], gradients[7], gradients[8])
```

```python
import functools

import jax
import jax.numpy as jnp
from jax import lax
from jax.experimental import pallas as pl
from jax.experimental.pallas import tpu as pltpu
from jax.sharding import PartitionSpec as P

MESH = pl.DeviceIdType.MESH

HDIM = 128
WIN = 2
BLOCK = 128
CAP = 128


EPSILON = 1e-05
ROPE_BASE = 10000.0
NEGATIVE = -1e30


def ring_place(index, count):
    if count != 8:
        return index
    z, y = index // 2, index % 2
    return z + y * (7 - 2 * z)


def ring_index(place, count):
    place = lax.rem(place + 2 * count, count)
    if count != 8:
        return place
    y = place // 4
    z = place - y * (2 * place - 7)
    return z * 2 + y


def ring_kernel(count, parts, *refs):
    ins, outs, slots = refs[:parts], refs[parts : 2 * parts], refs[2 * parts : 3 * parts]
    send_sem, recv_sem = refs[3 * parts :]
    me = ring_place(lax.axis_index("dp"), count)
    tensor = lax.axis_index("tensor")
    ahead = (
        (ring_index(me + 1, count), tensor),
        (ring_index(me - 1, count), tensor),
    )
    barrier = pltpu.get_barrier_semaphore()
    for device in ahead:
        pl.semaphore_signal(barrier, inc=1, device_id=device, device_id_type=MESH)
    pl.semaphore_wait(barrier, 2)

    def block(part, way, number):
        rows = ins[part].shape[1] // count
        half = ins[part].shape[2] // 2
        number = lax.rem(number + 2 * count, count)
        start = pl.multiple_of(number * rows, rows)
        return (slice(None), pl.ds(start, rows), pl.ds(way * half, half))

    def scatter_copy(part, way, step, source):
        return pltpu.make_async_remote_copy(
            src_ref=source,
            dst_ref=slots[part].at[way, step],
            send_sem=send_sem.at[0, way, step, part],
            recv_sem=recv_sem.at[0, way, step, part],
            device_id=ahead[way],
            device_id_type=MESH,
        )

    def gather_copy(part, way, step, number):
        where = outs[part].at[block(part, way, number)]
        return pltpu.make_async_remote_copy(
            src_ref=where,
            dst_ref=where,
            send_sem=send_sem.at[1, way, step, part],
            recv_sem=recv_sem.at[1, way, step, part],
            device_id=ahead[way],
            device_id_type=MESH,
        )

    both = [(part, way) for part in range(parts) for way in (0, 1)]
    sign = (1, -1)
    for part, way in both:
        scatter_copy(part, way, 0, ins[part].at[block(part, way, me)]).start()

    def add_own(part, way, step, target):
        where = block(part, way, me - sign[way] * (step + 1))
        depth, rows = ins[part].shape[0], ins[part].shape[1] // count
        piece = min(rows, 32)
        for layer in range(depth):

            @pl.loop(0, rows // piece)
            def _(turn):
                here = pl.ds(pl.multiple_of(turn * piece, piece), piece)
                mine = ins[part].at[where].at[layer, here, :]
                came = slots[part].at[way, step, layer, here, :]
                total = mine[...].astype(jnp.float32) + came[...].astype(jnp.float32)
                target.at[layer, here, :][...] = total.astype(jnp.bfloat16)

    @pl.loop(0, count - 2)
    def _(step):
        for part, way in both:
            source = slots[part].at[way, step]
            scatter_copy(part, way, step, source).wait_recv()
            add_own(part, way, step, source)
            scatter_copy(part, way, step + 1, source).start()

    last = count - 2
    for part, way in both:
        scatter_copy(part, way, last, slots[part].at[way, last]).wait_recv()
        mine = me + sign[way]
        add_own(part, way, last, outs[part].at[block(part, way, mine)])
        gather_copy(part, way, 0, mine).start()

    @pl.loop(0, count - 2)
    def _(step):
        for part, way in both:
            number = me - sign[way] * step
            gather_copy(part, way, step, number).wait_recv()
            gather_copy(part, way, step + 1, number).start()

    for part, way in both:
        gather_copy(part, way, last, me - sign[way] * last).wait_recv()

    @pl.loop(0, count - 1)
    def _(step):
        for part, way in both:
            scatter_copy(part, way, step, slots[part].at[way, step]).wait_send()
            gather_copy(part, way, step, me + sign[way] * (1 - step)).wait_send()


def ring_sum(arrays, count, number):
    parts = len(arrays)
    slots = [
        pltpu.VMEM((2, count - 1, a.shape[0], a.shape[1] // count, a.shape[2] // 2), jnp.bfloat16)
        for a in arrays
    ]
    sems = pltpu.SemaphoreType.DMA((2, 2, count - 1, parts))
    return pl.pallas_call(
        functools.partial(ring_kernel, count, parts),
        out_shape=[jax.ShapeDtypeStruct(a.shape, jnp.bfloat16) for a in arrays],
        in_specs=[pl.BlockSpec(memory_space=pltpu.VMEM)] * parts,
        out_specs=[pl.BlockSpec(memory_space=pltpu.VMEM)] * parts,
        scratch_shapes=[*slots, sems, sems],
        compiler_params=pltpu.CompilerParams(
            collective_id=number, has_side_effects=True, vmem_limit_bytes=60 << 20
        ),
        name="ring_sum",
    )(*arrays)


def row_scale(values):
    return lax.rsqrt(jnp.mean(values * values, axis=-1, keepdims=True) + EPSILON)


def rotate(values, positions):
    half_dim = values.shape[-1] // 2
    inv_freq = ROPE_BASE ** (-(jnp.arange(half_dim, dtype=jnp.float32) * 2.0) / values.shape[-1])
    turn_angle = positions.astype(jnp.float32)[:, None] * inv_freq[None, :]
    cosine = jnp.cos(turn_angle)[:, None, :]
    sine_vals = jnp.sin(turn_angle)[:, None, :]
    first_half = values[..., :half_dim]
    second_half = values[..., half_dim:]
    return jnp.concatenate(
        [
            first_half * cosine - second_half * sine_vals,
            second_half * cosine + first_half * sine_vals,
        ],
        axis=-1,
    )


def token_tables(seq_blocks, block_place, row_ids):
    block_total = block_place.shape[0]
    seq_total = seq_blocks.shape[0]
    seq_ends = jnp.cumsum(seq_blocks)
    seq_firsts = seq_ends - seq_blocks
    given_block = row_ids // BLOCK
    packed = jnp.sum(
        jnp.where(
            given_block[:, None] == jnp.arange(block_total, dtype=jnp.int32)[None, :],
            block_place[None, :],
            0,
        ),
        axis=1,
    )
    seq_of = jnp.sum((packed[:, None] >= seq_ends[None, :]).astype(jnp.int32), axis=1)
    first_of = jnp.sum(
        jnp.where(
            seq_of[:, None] == jnp.arange(seq_total, dtype=jnp.int32)[None, :],
            seq_firsts[None, :],
            0,
        ),
        axis=1,
    )
    return (seq_of, (packed - first_of) * BLOCK + row_ids % BLOCK)


def norm_back(values, row_factor, gain_row, incoming, model_width):
    scaled = gain_row * incoming
    inner_sum = jnp.sum(scaled * values, axis=-1, keepdims=True)
    return row_factor * scaled - values * (row_factor**3 / model_width) * inner_sum


def masked_scores(query_rows, seg_rows, pos_rows, key_rows, seg_cols, pos_cols, keep_cols):
    raw_scores = jnp.einsum(
        "qhd,khd->hqk", query_rows, key_rows, preferred_element_type=jnp.float32
    )
    allowed = (
        (seg_rows[:, None] == seg_cols[None, :])
        & (pos_cols[None, :] <= pos_rows[:, None])
        & (keep_cols[None, :] > 0)
    )
    return jnp.where(allowed[None], raw_scores * HDIM ** (-0.5), NEGATIVE)


def score_grads(
    query_rows,
    seg_rows,
    pos_rows,
    top_rows,
    shift_rows,
    du_rows,
    key_rows,
    value_rows,
    seg_cols,
    pos_cols,
    keep_cols,
):
    weights = jnp.exp(
        masked_scores(query_rows, seg_rows, pos_rows, key_rows, seg_cols, pos_cols, keep_cols)
        - top_rows[:, :, None]
    )
    value_dots = jnp.einsum("qhd,khd->hqk", du_rows, value_rows, preferred_element_type=jnp.float32)
    score_grad = (weights * (value_dots - shift_rows[:, :, None]) * HDIM ** (-0.5)).astype(
        jnp.bfloat16
    )
    return (weights.astype(jnp.bfloat16), score_grad)


def body(
    tokens,
    seq_blocks,
    block_place,
    pad_mask,
    expert_ids,
    attn_gain,
    w_qkv,
    qk_gain,
    w_out,
    ffn_gain,
    router,
    expert_in,
    expert_out,
    cotangent,
):
    rows_here = tokens.shape[0]
    model_width = tokens.shape[1]
    local_width = w_qkv.shape[2]
    heads_here = local_width // HDIM
    local_ff = expert_out.shape[1]
    tensor_index = lax.axis_index("tensor")
    feature_start = tensor_index * local_width
    first_row = lax.axis_index("dp") * rows_here
    row_ids = first_row + jnp.arange(rows_here, dtype=jnp.int32)
    seg_q, pos_q = token_tables(seq_blocks, block_place, row_ids)
    inputs = tokens.astype(jnp.float32)
    x_scale = row_scale(inputs)
    normed_in = (inputs * x_scale * attn_gain).astype(jnp.bfloat16)
    projected = jnp.dot(
        normed_in, w_qkv.reshape(model_width, 3 * local_width), preferred_element_type=jnp.float32
    ).reshape(rows_here, 3, local_width)
    queries = projected[:, 0]
    keys_here = projected[:, 1]
    values_here = projected[:, 2]
    sums_q, sums_k = lax.psum(
        (jnp.sum(queries * queries, axis=-1), jnp.sum(keys_here * keys_here, axis=-1)), "tensor"
    )
    q_scale = lax.rsqrt(sums_q / model_width + EPSILON)[:, None]
    k_scale = lax.rsqrt(sums_k / model_width + EPSILON)[:, None]
    q_norm = (queries * q_scale * qk_gain[0]).reshape(rows_here, heads_here, HDIM)
    k_norm = (keys_here * k_scale * qk_gain[1]).reshape(rows_here, heads_here, HDIM)
    q_rot = rotate(q_norm, pos_q).astype(jnp.bfloat16)
    k_rot = rotate(k_norm, pos_q).astype(jnp.bfloat16)
    v_low = values_here.astype(jnp.bfloat16)
    keep_here = pad_mask.astype(jnp.bfloat16)
    k_all, v_all, keep_all = (
        lax.all_gather(k_rot.reshape(rows_here, local_width), "dp", axis=0, tiled=True),
        lax.all_gather(v_low, "dp", axis=0, tiled=True),
        lax.all_gather(keep_here, "dp", axis=0, tiled=True),
    )
    total_rows = k_all.shape[0]
    all_ids = jnp.arange(total_rows, dtype=jnp.int32)
    seg_keys, pos_keys = token_tables(seq_blocks, block_place, all_ids)
    key_block = min(1024, total_rows)
    block_count = total_rows // key_block
    keys_blocks = k_all.reshape(block_count, key_block, heads_here, HDIM)
    values_blocks = v_all.reshape(block_count, key_block, heads_here, HDIM)
    seg_blocks = seg_keys.reshape(block_count, key_block)
    pos_blocks = pos_keys.reshape(block_count, key_block)
    keep_blocks = keep_all.reshape(block_count, key_block)

    def online_step(carry_state, block_in):
        run_top, row_acc, value_acc = carry_state
        keys_b, values_b, seg_b, pos_b, keep_b = block_in
        found = masked_scores(q_rot, seg_q, pos_q, keys_b, seg_b, pos_b, keep_b)
        new_top = jnp.maximum(run_top, jnp.max(found, axis=-1))
        factor = jnp.exp(run_top - new_top)
        weights = jnp.exp(found - new_top[:, :, None])
        row_acc = row_acc * factor + jnp.sum(weights, axis=-1)
        value_acc = value_acc * jnp.transpose(factor)[:, :, None] + jnp.einsum(
            "hqk,khd->qhd",
            weights.astype(jnp.bfloat16),
            values_b,
            preferred_element_type=jnp.float32,
        )
        return ((new_top, row_acc, value_acc), None)

    start_state = (
        jnp.full((heads_here, rows_here), NEGATIVE, jnp.float32),
        jnp.zeros((heads_here, rows_here), jnp.float32),
        jnp.zeros((rows_here, heads_here, HDIM), jnp.float32),
    )
    (row_top, row_sum, value_sum), _ = lax.scan(
        online_step, start_state, (keys_blocks, values_blocks, seg_blocks, pos_blocks, keep_blocks)
    )
    attended = value_sum / jnp.transpose(row_sum)[:, :, None]
    attended_low = attended.astype(jnp.bfloat16).reshape(rows_here, local_width)
    branch = lax.psum(
        jnp.dot(attended_low, w_out, preferred_element_type=jnp.float32).astype(jnp.bfloat16),
        "tensor",
    ).astype(jnp.float32)
    hidden = inputs + branch
    h_scale = row_scale(hidden)
    normed = (hidden * h_scale * ffn_gain).astype(jnp.bfloat16)
    logits = jnp.dot(normed, router, preferred_element_type=jnp.float32)
    router_probs = jax.nn.softmax(logits, axis=-1)
    window_ids = jnp.arange(WIN, dtype=jnp.int32)
    chosen = jnp.any(expert_ids[:, :, None] == window_ids[None, None, :], axis=1)
    chosen_float = chosen.astype(jnp.float32)
    gate_values = router_probs[:, :WIN] * chosen_float
    slot_ids = jnp.arange(CAP, dtype=jnp.int32)
    token_ids = jnp.arange(rows_here, dtype=jnp.int32)
    mixture = jnp.zeros((rows_here, model_width), jnp.float32)
    saved_slots = []
    for expert in range(WIN):
        picked = chosen[:, expert]
        slot_rank = jnp.cumsum(picked.astype(jnp.int32)) - 1
        slot_table = (slot_rank[None, :] == slot_ids[:, None]) & picked[None, :]
        slot_token = jnp.sum(jnp.where(slot_table, token_ids[None, :], 0), axis=1)
        slot_live = jnp.any(slot_table, axis=1).astype(jnp.float32)
        gathered_rows = jnp.take(normed, slot_token, axis=0)
        gate_up = jnp.dot(
            gathered_rows,
            expert_in[expert].reshape(model_width, 2 * local_ff),
            preferred_element_type=jnp.float32,
        ).reshape(CAP, 2, local_ff)
        active = (jax.nn.silu(gate_up[:, 0]) * gate_up[:, 1]).astype(jnp.bfloat16)
        expert_part = jnp.dot(active, expert_out[expert], preferred_element_type=jnp.float32)
        slot_gate = jnp.take(gate_values[:, expert], slot_token) * slot_live
        mixture = mixture.at[slot_token].add(slot_gate[:, None] * expert_part)
        saved_slots.append(
            (slot_token, slot_live, gathered_rows, gate_up, active, expert_part, slot_gate)
        )
    mixture_share = lax.psum_scatter(
        mixture.astype(jnp.bfloat16), "tensor", scatter_dimension=1, tiled=True
    ).astype(jnp.float32)
    hidden_share = lax.dynamic_slice_in_dim(hidden, feature_start, local_width, 1)
    output = (hidden_share + mixture_share).astype(jnp.bfloat16)
    cot_full = lax.all_gather(cotangent, "tensor", axis=1, tiled=True).astype(jnp.float32)
    mixture_grad = jnp.zeros((rows_here, model_width), jnp.float32)
    gate_columns = []
    expert_in_list = []
    expert_out_list = []
    for expert in range(WIN):
        slot_token, slot_live, gathered_rows, gate_up, active, expert_part, slot_gate = saved_slots[
            expert
        ]
        cot_rows = jnp.take(cot_full, slot_token, axis=0)
        part_grad = (slot_gate[:, None] * cot_rows).astype(jnp.bfloat16)
        slot_dots = jnp.sum(cot_rows * expert_part, axis=-1) * slot_live
        gate_columns.append(jnp.zeros((rows_here,), jnp.float32).at[slot_token].add(slot_dots))
        expert_out_list.append(
            jnp.einsum("cf,cd->fd", active, part_grad, preferred_element_type=jnp.float32)
        )
        active_grad = jnp.einsum(
            "cd,fd->cf", part_grad, expert_out[expert], preferred_element_type=jnp.float32
        )
        _, silu_pull = jax.vjp(
            lambda gate_in, up_in: jax.nn.silu(gate_in) * up_in, gate_up[:, 0], gate_up[:, 1]
        )
        gate_in_grad, up_in_grad = silu_pull(active_grad)
        pair_grad = (
            jnp.stack([gate_in_grad, up_in_grad], axis=1)
            .astype(jnp.bfloat16)
            .reshape(CAP, 2 * local_ff)
        )
        expert_in_list.append(
            jnp.einsum(
                "cd,cf->df", gathered_rows, pair_grad, preferred_element_type=jnp.float32
            ).reshape(model_width, 2, local_ff)
        )
        row_grad = jnp.einsum(
            "cf,df->cd",
            pair_grad,
            expert_in[expert].reshape(model_width, 2 * local_ff),
            preferred_element_type=jnp.float32,
        )
        mixture_grad = mixture_grad.at[slot_token].add(row_grad)
    gate_grad = jnp.stack(gate_columns, axis=1)
    mixture_grad, gate_grad = (
        lax.psum(mixture_grad.astype(jnp.bfloat16), "tensor").astype(jnp.float32),
        lax.psum(gate_grad.astype(jnp.bfloat16), "tensor").astype(jnp.float32),
    )
    probs_grad = jnp.concatenate(
        [gate_grad * chosen_float, jnp.zeros((rows_here, router.shape[1] - WIN), jnp.float32)],
        axis=1,
    )
    logit_grad = (
        router_probs * (probs_grad - jnp.sum(router_probs * probs_grad, axis=-1, keepdims=True))
    ).astype(jnp.bfloat16)
    normed_grad = mixture_grad + jnp.einsum(
        "te,de->td", logit_grad, router, preferred_element_type=jnp.float32
    )
    normed_share = lax.dynamic_slice_in_dim(normed, feature_start, local_width, 1)
    router_grad = jnp.einsum(
        "td,te->de", normed_share, logit_grad, preferred_element_type=jnp.float32
    )
    ffn_gain_grad = lax.dynamic_slice_in_dim(
        jnp.sum(normed_grad * hidden * h_scale, axis=0), feature_start, local_width, 0
    )
    hidden_grad = cot_full + norm_back(hidden, h_scale, ffn_gain, normed_grad, model_width)
    expert_in_grad = jnp.stack(expert_in_list)
    expert_out_grad = jnp.stack(expert_out_list)
    branch_grad = hidden_grad.astype(jnp.bfloat16)
    out_grad = jnp.einsum(
        "tc,td->cd", attended_low, branch_grad, preferred_element_type=jnp.float32
    )
    attended_grad = (
        jnp.einsum("td,cd->tc", branch_grad, w_out, preferred_element_type=jnp.float32)
        .astype(jnp.bfloat16)
        .reshape(rows_here, heads_here, HDIM)
    )
    grad_wide = attended_grad.astype(jnp.float32)
    delta_rows = jnp.transpose(jnp.sum(grad_wide * attended, axis=-1))
    scaled_grad = (grad_wide / jnp.transpose(row_sum)[:, :, None]).astype(jnp.bfloat16)
    shift_rows = delta_rows / row_sum

    def key_step(carry_sum, block_in):
        keys_b, values_b, seg_b, pos_b, keep_b = block_in
        low_weights, score_grad = score_grads(
            q_rot,
            seg_q,
            pos_q,
            row_top,
            shift_rows,
            scaled_grad,
            keys_b,
            values_b,
            seg_b,
            pos_b,
            keep_b,
        )
        carry_sum = carry_sum + jnp.einsum(
            "hqk,khd->qhd", score_grad, keys_b, preferred_element_type=jnp.float32
        )
        key_term = jnp.einsum("hqk,qhd->khd", score_grad, q_rot, preferred_element_type=jnp.float32)
        value_term = jnp.einsum(
            "hqk,qhd->khd", low_weights, scaled_grad, preferred_element_type=jnp.float32
        )
        return (
            carry_sum,
            jnp.concatenate(
                [
                    key_term.reshape(key_block, local_width),
                    value_term.reshape(key_block, local_width),
                ],
                axis=1,
            ),
        )

    query_grad, kv_terms = lax.scan(
        key_step,
        jnp.zeros((rows_here, heads_here, HDIM), jnp.float32),
        (keys_blocks, values_blocks, seg_blocks, pos_blocks, keep_blocks),
    )
    kv_grad = lax.psum_scatter(
        kv_terms.reshape(total_rows, 2 * local_width).astype(jnp.bfloat16),
        "dp",
        scatter_dimension=0,
        tiled=True,
    ).astype(jnp.float32)
    key_grad = kv_grad[:, :local_width]
    value_grad = kv_grad[:, local_width:]
    value_low_grad = value_grad.astype(jnp.bfloat16)
    _, rope_pull = jax.vjp(lambda turned: rotate(turned, pos_q), q_norm)
    q_norm_grad = rope_pull(query_grad)[0].reshape(rows_here, local_width)
    k_norm_grad = rope_pull(key_grad.reshape(rows_here, heads_here, HDIM))[0].reshape(
        rows_here, local_width
    )
    scaled_q = qk_gain[0] * q_norm_grad
    scaled_k = qk_gain[1] * k_norm_grad
    inner_q, inner_k = lax.psum(
        (jnp.sum(scaled_q * queries, axis=-1), jnp.sum(scaled_k * keys_here, axis=-1)), "tensor"
    )
    q_grad = (
        q_scale * scaled_q - queries * (q_scale**3 / model_width) * inner_q[:, None]
    ).astype(jnp.bfloat16)
    k_grad = (
        k_scale * scaled_k - keys_here * (k_scale**3 / model_width) * inner_k[:, None]
    ).astype(jnp.bfloat16)
    qk_gain_grad = jnp.stack(
        [
            jnp.sum(q_norm_grad * queries * q_scale, axis=0),
            jnp.sum(k_norm_grad * keys_here * k_scale, axis=0),
        ]
    )
    proj_grad = jnp.stack([q_grad, k_grad, value_low_grad], axis=1).reshape(
        rows_here, 3 * local_width
    )
    qkv_grad = jnp.einsum(
        "td,tc->dc", normed_in, proj_grad, preferred_element_type=jnp.float32
    ).reshape(model_width, 3, local_width)
    normed_in_grad = jnp.einsum(
        "tc,dc->td",
        proj_grad,
        w_qkv.reshape(model_width, 3 * local_width),
        preferred_element_type=jnp.float32,
    )
    input_part = norm_back(inputs, x_scale, attn_gain, normed_in_grad, model_width)
    gain_part = jnp.sum(normed_in_grad * inputs * x_scale, axis=0)
    input_sum, attn_gain_grad = (
        lax.psum_scatter(
            input_part.astype(jnp.bfloat16), "tensor", scatter_dimension=1, tiled=True
        ).astype(jnp.float32),
        lax.psum_scatter(
            gain_part.astype(jnp.bfloat16), "tensor", scatter_dimension=0, tiled=True
        ).astype(jnp.float32),
    )
    input_grad = (
        lax.dynamic_slice_in_dim(hidden_grad, feature_start, local_width, 1) + input_sum
    ).astype(jnp.bfloat16)
    dp_count = lax.axis_size("dp")
    small = jnp.concatenate(
        [
            router_grad.reshape(-1, 256),
            jnp.concatenate([attn_gain_grad, ffn_gain_grad, qk_gain_grad.reshape(-1)]).reshape(
                -1, 256
            ),
        ]
    ).astype(jnp.bfloat16)
    small_rows = small.shape[0]
    small = jnp.pad(small, ((0, -small_rows % (dp_count * 8)), (0, 0)))
    low = jnp.bfloat16
    qkv_sum, out_sum, in_sum, exp_sum, small_sum = ring_sum(
        [
            jnp.transpose(qkv_grad, (1, 0, 2)).astype(low),
            out_grad.astype(low)[None],
            expert_in_grad.reshape(WIN, model_width, 2 * local_ff).astype(low),
            expert_out_grad.astype(low),
            small[None],
        ],
        dp_count,
        0,
    )
    qkv_grad = jnp.transpose(qkv_sum.astype(jnp.float32), (1, 0, 2))
    out_grad = out_sum[0].astype(jnp.float32)
    expert_in_grad = in_sum.astype(jnp.float32).reshape(expert_in_grad.shape)
    expert_out_grad = exp_sum.astype(jnp.float32)
    router_rows = router_grad.size // 256
    small_sum = small_sum[0].astype(jnp.float32)
    router_grad = small_sum[:router_rows].reshape(router_grad.shape)
    gains = small_sum[router_rows:small_rows].reshape(-1)
    attn_gain_grad = gains[:local_width]
    ffn_gain_grad = gains[local_width : 2 * local_width]
    qk_gain_grad = gains[2 * local_width :].reshape(2, local_width)
    return (
        output,
        input_grad,
        attn_gain_grad,
        qkv_grad,
        qk_gain_grad,
        out_grad,
        ffn_gain_grad,
        router_grad,
        expert_in_grad,
        expert_out_grad,
    )


def solution(mesh):
    placed = (
        P("dp", None),
        P(),
        P(),
        P("dp"),
        P("dp", None),
        P(),
        P(None, None, "tensor"),
        P(None, "tensor"),
        P("tensor", None),
        P(),
        P(),
        P(None, None, None, "tensor"),
        P(None, "tensor", None),
        P("dp", "tensor"),
    )
    return jax.shard_map(
        body,
        mesh=mesh,
        in_specs=placed,
        out_specs=(
            P("dp", "tensor"),
            P("dp", "tensor"),
            P("tensor"),
            P(None, None, "tensor"),
            P(None, "tensor"),
            P("tensor", None),
            P("tensor"),
            P("tensor", None),
            P(None, None, None, "tensor"),
            P(None, "tensor", None),
        ),
        check_vma=False,
    )
```

```python
import functools

import jax
import jax.numpy as jnp
from jax import lax
from jax.experimental import pallas as pl
from jax.experimental.pallas import tpu as pltpu
from jax.sharding import PartitionSpec as P

MESH = pl.DeviceIdType.MESH

HDIM = 128
WIN = 2
BLOCK = 128
CAP = 128


EPSILON = 1e-05
ROPE_BASE = 10000.0
NEGATIVE = -1e30
LOG2E = 1.4426950408889634
TILE = 512


def ring_place(index, count):
    if count != 8:
        return index
    z, y = index // 2, index % 2
    return z + y * (7 - 2 * z)


def ring_index(place, count):
    place = lax.rem(place + 2 * count, count)
    if count != 8:
        return place
    y = place // 4
    z = place - y * (2 * place - 7)
    return z * 2 + y


def ring_kernel(count, parts, *refs):
    ins, outs, slots = refs[:parts], refs[parts : 2 * parts], refs[2 * parts : 3 * parts]
    send_sem, recv_sem = refs[3 * parts :]
    me = ring_place(lax.axis_index("dp"), count)
    tensor = lax.axis_index("tensor")
    ahead = (
        (ring_index(me + 1, count), tensor),
        (ring_index(me - 1, count), tensor),
    )
    barrier = pltpu.get_barrier_semaphore()
    for device in ahead:
        pl.semaphore_signal(barrier, inc=1, device_id=device, device_id_type=MESH)
    pl.semaphore_wait(barrier, 2)

    def block(part, way, number):
        rows = ins[part].shape[1] // count
        half = ins[part].shape[2] // 2
        number = lax.rem(number + 2 * count, count)
        start = pl.multiple_of(number * rows, rows)
        return (slice(None), pl.ds(start, rows), pl.ds(way * half, half))

    def scatter_copy(part, way, step, source):
        return pltpu.make_async_remote_copy(
            src_ref=source,
            dst_ref=slots[part].at[way, step],
            send_sem=send_sem.at[0, way, step, part],
            recv_sem=recv_sem.at[0, way, step, part],
            device_id=ahead[way],
            device_id_type=MESH,
        )

    def gather_copy(part, way, step, number):
        where = outs[part].at[block(part, way, number)]
        return pltpu.make_async_remote_copy(
            src_ref=where,
            dst_ref=where,
            send_sem=send_sem.at[1, way, step, part],
            recv_sem=recv_sem.at[1, way, step, part],
            device_id=ahead[way],
            device_id_type=MESH,
        )

    both = [(part, way) for part in range(parts) for way in (0, 1)]
    sign = (1, -1)
    for part, way in both:
        scatter_copy(part, way, 0, ins[part].at[block(part, way, me)]).start()

    def add_own(part, way, step, target):
        where = block(part, way, me - sign[way] * (step + 1))
        depth, rows = ins[part].shape[0], ins[part].shape[1] // count
        piece = min(rows, 32)
        for layer in range(depth):

            @pl.loop(0, rows // piece)
            def _(turn):
                here = pl.ds(pl.multiple_of(turn * piece, piece), piece)
                mine = ins[part].at[where].at[layer, here, :]
                came = slots[part].at[way, step, layer, here, :]
                total = mine[...].astype(jnp.float32) + came[...].astype(jnp.float32)
                target.at[layer, here, :][...] = total.astype(jnp.bfloat16)

    @pl.loop(0, count - 2)
    def _(step):
        for part, way in both:
            source = slots[part].at[way, step]
            scatter_copy(part, way, step, source).wait_recv()
            add_own(part, way, step, source)
            scatter_copy(part, way, step + 1, source).start()

    last = count - 2
    for part, way in both:
        scatter_copy(part, way, last, slots[part].at[way, last]).wait_recv()
        mine = me + sign[way]
        add_own(part, way, last, outs[part].at[block(part, way, mine)])
        gather_copy(part, way, 0, mine).start()

    @pl.loop(0, count - 2)
    def _(step):
        for part, way in both:
            number = me - sign[way] * step
            gather_copy(part, way, step, number).wait_recv()
            gather_copy(part, way, step + 1, number).start()

    for part, way in both:
        gather_copy(part, way, last, me - sign[way] * last).wait_recv()

    @pl.loop(0, count - 1)
    def _(step):
        for part, way in both:
            scatter_copy(part, way, step, slots[part].at[way, step]).wait_send()
            gather_copy(part, way, step, me + sign[way] * (1 - step)).wait_send()


def ring_sum(arrays, count, number):
    parts = len(arrays)
    slots = [
        pltpu.VMEM((2, count - 1, a.shape[0], a.shape[1] // count, a.shape[2] // 2), jnp.bfloat16)
        for a in arrays
    ]
    sems = pltpu.SemaphoreType.DMA((2, 2, count - 1, parts))
    return pl.pallas_call(
        functools.partial(ring_kernel, count, parts),
        out_shape=[jax.ShapeDtypeStruct(a.shape, jnp.bfloat16) for a in arrays],
        in_specs=[pl.BlockSpec(memory_space=pltpu.VMEM)] * parts,
        out_specs=[pl.BlockSpec(memory_space=pltpu.VMEM)] * parts,
        scratch_shapes=[*slots, sems, sems],
        compiler_params=pltpu.CompilerParams(
            collective_id=number, has_side_effects=True, vmem_limit_bytes=60 << 20
        ),
        name="ring_sum",
    )(*arrays)


def line_place(count, heads):
    me = lax.axis_index("dp")
    across = count // heads
    return me // across, lax.rem(me, across), across


def greet(devices):
    barrier = pltpu.get_barrier_semaphore()
    for device in devices:
        pl.semaphore_signal(barrier, inc=1, device_id=device, device_id_type=MESH)
    pl.semaphore_wait(barrier, len(devices))


def line_devices(count, heads):
    z, w, across = line_place(count, heads)
    tensor = lax.axis_index("tensor")
    along = [(lax.rem(z + dz, heads) * across + w, tensor) for dz in range(1, heads)]
    beside = [(z * across + lax.rem(w + dw, across), tensor) for dw in range(1, across)]
    return along, beside


def head_columns(number):
    return (slice(None), pl.ds(pl.multiple_of(number * HDIM, HDIM), HDIM))


def spread_kernel(count, heads, q, k, v, keep, q_all, k_all, v_all, keep_all, *sems):
    send_one, recv_one, send_two, recv_two, near = sems
    z, w, across = line_place(count, heads)
    me = z * across + w
    along, beside = line_devices(count, heads)
    greet(along + beside)
    pairs = ((k, k_all), (v, v_all), (keep, keep_all), (q, q_all))

    def piece(item, head):
        source = pairs[item][0]
        return source if item == 2 else source.at[head_columns(head)]

    def first_copy(item, dz):
        head = lax.rem(z + dz, heads)
        return pltpu.make_async_remote_copy(
            src_ref=piece(item, head),
            dst_ref=pairs[item][1].at[z if item == 3 else me],
            send_sem=send_one.at[item, dz - 1],
            recv_sem=recv_one.at[item, dz - 1],
            device_id=along[dz - 1],
            device_id_type=MESH,
        )

    def second_copy(item, dz, dw):
        where = lax.rem(z - dz + heads, heads) * across + w
        return pltpu.make_async_remote_copy(
            src_ref=piece(item, z) if dz == 0 else pairs[item][1].at[where],
            dst_ref=pairs[item][1].at[where],
            send_sem=send_two.at[item, dz, dw - 1],
            recv_sem=recv_two.at[item, dz, dw - 1],
            device_id=beside[dw - 1],
            device_id_type=MESH,
        )

    first = [(item, dz) for dz in range(1, heads) for item in range(4)]
    second = [(dz, item, dw) for dz in range(heads) for item in range(3) for dw in range(1, across)]
    local = []
    for item, dz in first:
        first_copy(item, dz).start()
    for dz, item, dw in second:
        if dz == 0:
            second_copy(item, dz, dw).start()
    for item in range(4):
        own = pairs[item][1].at[z if item == 3 else me]
        copy = pltpu.make_async_copy(piece(item, z), own, near.at[item])
        copy.start()
        local.append(copy)
    for item, dz in first:
        first_copy(item, dz).wait_recv()
        if item < 3:
            for dw in range(1, across):
                second_copy(item, dz, dw).start()
    for dz, item, dw in second:
        second_copy(item, dz, dw).wait_recv()
    for item, dz in first:
        first_copy(item, dz).wait_send()
    for dz, item, dw in second:
        second_copy(item, dz, dw).wait_send()
    for copy in local:
        copy.wait()


def spread_heads(q, k, v, keep, count, heads, number):
    rows = q.shape[0]
    across = count // heads
    sem = pltpu.SemaphoreType.DMA
    shapes = [(heads, rows, HDIM), (count, rows, HDIM), (count, rows, HDIM), (count, *keep.shape)]
    return pl.pallas_call(
        functools.partial(spread_kernel, count, heads),
        out_shape=[jax.ShapeDtypeStruct(shape, jnp.bfloat16) for shape in shapes],
        in_specs=[pl.BlockSpec(memory_space=pl.ANY)] * 4,
        out_specs=[pl.BlockSpec(memory_space=pl.ANY)] * 4,
        scratch_shapes=[
            sem((4, heads - 1)),
            sem((4, heads - 1)),
            sem((3, heads, across - 1)),
            sem((3, heads, across - 1)),
            sem((4,)),
        ],
        compiler_params=pltpu.CompilerParams(collective_id=number, has_side_effects=True),
        name="spread_heads",
    )(q, k, v, keep)


def swap_kernel(count, heads, join, source, result, send_sem, recv_sem, near):
    z, w, across = line_place(count, heads)
    along, _ = line_devices(count, heads)
    greet(along)

    def copy_to(dz):
        far = lax.rem(z + dz, heads)
        return pltpu.make_async_remote_copy(
            src_ref=source.at[far] if join else source.at[head_columns(far)],
            dst_ref=result.at[head_columns(z)] if join else result.at[z],
            send_sem=send_sem.at[dz - 1],
            recv_sem=recv_sem.at[dz - 1],
            device_id=along[dz - 1],
            device_id_type=MESH,
        )

    for dz in range(1, heads):
        copy_to(dz).start()
    own = pltpu.make_async_copy(
        source.at[z] if join else source.at[head_columns(z)],
        result.at[head_columns(z)] if join else result.at[z],
        near,
    )
    own.start()
    for dz in range(1, heads):
        copy_to(dz).wait()
    own.wait()


def swap_line(source, count, heads, join, number):
    rows = source.shape[1] if join else source.shape[0]
    shape = (rows, heads * HDIM) if join else (heads, rows, HDIM)
    sem = pltpu.SemaphoreType.DMA
    return pl.pallas_call(
        functools.partial(swap_kernel, count, heads, join),
        out_shape=jax.ShapeDtypeStruct(shape, jnp.bfloat16),
        in_specs=[pl.BlockSpec(memory_space=pl.ANY)],
        out_specs=pl.BlockSpec(memory_space=pl.ANY),
        scratch_shapes=[sem((heads - 1,)), sem((heads - 1,)), sem],
        compiler_params=pltpu.CompilerParams(collective_id=number, has_side_effects=True),
        name="join_heads" if join else "part_heads",
    )(source)


def return_kernel(count, heads, dq, dk, dv, dq_own, dk_own, dv_own, came_k, came_v, total_k, total_v, *sems):
    send_one, recv_one, send_two, recv_two, near = sems
    z, w, across = line_place(count, heads)
    along, beside = line_devices(count, heads)
    greet(along + beside)
    partial = ((dk, came_k, total_k), (dv, came_v, total_v))
    whole = (dk_own, dv_own, dq_own)
    lines = [lax.rem(z + dz, heads) for dz in (*range(1, heads), 0)]

    def first_copy(item, turn, dw):
        return pltpu.make_async_remote_copy(
            src_ref=partial[item][0].at[lines[turn] * across + lax.rem(w + dw, across)],
            dst_ref=partial[item][1].at[turn, dw - 1],
            send_sem=send_one.at[item, turn, dw - 1],
            recv_sem=recv_one.at[item, turn, dw - 1],
            device_id=beside[dw - 1],
            device_id_type=MESH,
        )

    def second_copy(item, turn):
        return pltpu.make_async_remote_copy(
            src_ref=dq.at[lines[turn]] if item == 2 else partial[item][2].at[turn],
            dst_ref=whole[item].at[head_columns(z)],
            send_sem=send_two.at[item, turn],
            recv_sem=recv_two.at[item, turn],
            device_id=along[turn],
            device_id_type=MESH,
        )

    def landed(item, turn):
        back = lax.rem(z - turn - 1 + heads, heads)
        where = whole[item].at[head_columns(back)]
        return pltpu.make_async_remote_copy(
            src_ref=where,
            dst_ref=where,
            send_sem=send_two.at[item, turn],
            recv_sem=recv_two.at[item, turn],
            device_id=along[turn],
            device_id_type=MESH,
        )

    rows = dk.shape[1]
    piece = 128
    first = [(item, turn, dw) for turn in range(heads) for item in (0, 1) for dw in range(1, across)]
    for item, turn, dw in first:
        first_copy(item, turn, dw).start()
    for turn in range(heads - 1):
        second_copy(2, turn).start()
    local = [pltpu.make_async_copy(dq.at[z], dq_own.at[head_columns(z)], near.at[2])]
    local[0].start()
    for turn in range(heads):
        for item in (0, 1):
            own, came, total = partial[item]
            for dw in range(1, across):
                first_copy(item, turn, dw).wait_recv()

            @pl.loop(0, rows // piece)
            def _(part):
                here = pl.ds(pl.multiple_of(part * piece, piece), piece)
                result = own[lines[turn] * across + w, here, :].astype(jnp.float32)
                for dw in range(1, across):
                    result = result + came[turn, dw - 1, here, :].astype(jnp.float32)
                total[turn, here, :] = result.astype(jnp.bfloat16)

            if turn < heads - 1:
                second_copy(item, turn).start()
            else:
                copy = pltpu.make_async_copy(
                    total.at[turn], whole[item].at[head_columns(z)], near.at[item]
                )
                copy.start()
                local.append(copy)
    for item in range(3):
        for turn in range(heads - 1):
            landed(item, turn).wait_recv()
            second_copy(item, turn).wait_send()
    for item, turn, dw in first:
        first_copy(item, turn, dw).wait_send()
    for copy in local:
        copy.wait()


def return_heads(dq, dk, dv, count, heads, number):
    rows = dq.shape[1]
    across = count // heads
    sem = pltpu.SemaphoreType.DMA
    vmem = pl.BlockSpec(memory_space=pltpu.VMEM)
    came = pltpu.VMEM((heads, across - 1, rows, HDIM), jnp.bfloat16)
    total = pltpu.VMEM((heads, rows, HDIM), jnp.bfloat16)
    own = jax.ShapeDtypeStruct((rows, heads * HDIM), jnp.bfloat16)
    return pl.pallas_call(
        functools.partial(return_kernel, count, heads),
        out_shape=[own] * 3,
        in_specs=[vmem] * 3,
        out_specs=[vmem] * 3,
        scratch_shapes=[
            came,
            came,
            total,
            total,
            sem((2, heads, across - 1)),
            sem((2, heads, across - 1)),
            sem((3, heads - 1)),
            sem((3, heads - 1)),
            sem((3,)),
        ],
        compiler_params=pltpu.CompilerParams(
            collective_id=number, has_side_effects=True, vmem_limit_bytes=60 << 20
        ),
        name="return_heads",
    )(dq, dk, dv)


def across_rows(left, right):
    return lax.dot_general(
        left, right, (((1,), (1,)), ((), ())), preferred_element_type=jnp.float32
    )


def attend_kernel(inverse, first, own, stop, q, k, v, out, out_low, top, k_packed, v_turned):
    blocks = inverse.shape[0]
    rate = HDIM**-0.5 * LOG2E

    @pl.loop(0, blocks)
    def _(b):
        here = pl.ds(pl.multiple_of(b * BLOCK, BLOCK), BLOCK)
        there = pl.ds(pl.multiple_of(inverse[b] * BLOCK, BLOCK), BLOCK)
        k_packed[here, :] = k[there, :]
        v_turned[:, here] = v[there, :].T

    k_packed[blocks * BLOCK :, :] = jnp.zeros((TILE, HDIM), jnp.bfloat16)
    v_turned[:, blocks * BLOCK :] = jnp.zeros((HDIM, TILE), jnp.bfloat16)
    lane = lax.broadcasted_iota(jnp.int32, (1, BLOCK), 1)
    row = lax.broadcasted_iota(jnp.int32, (TILE, BLOCK), 0)

    @pl.loop(0, own.shape[0])
    def _(i):
        rows = pl.ds(pl.multiple_of(i * BLOCK, BLOCK), BLOCK)
        queries = q[rows, :]
        start = first[i]
        limit = jnp.minimum(own[i] * BLOCK + lane, stop[i] - 1)
        tiles = (own[i] - start) // (TILE // BLOCK) + 1

        def step(t, state):
            run_top, run_sum, run_out = state
            base = pl.multiple_of((start * BLOCK) + t * TILE, BLOCK)
            keys = pl.ds(base, TILE)
            found = across_rows(k_packed[keys, :], queries)
            found = jnp.where(row <= limit - base, found, NEGATIVE)
            new_top = jnp.maximum(run_top, jnp.max(found, axis=0, keepdims=True))
            factor = jnp.exp2((run_top - new_top) * rate)
            weights = jnp.exp2((found - new_top) * rate)
            run_sum = run_sum * factor + jnp.sum(weights, axis=0, keepdims=True)
            run_out = run_out * factor + jnp.dot(
                v_turned[:, keys],
                weights.astype(jnp.bfloat16),
                preferred_element_type=jnp.float32,
            )
            return new_top, run_sum, run_out

        new_top, run_sum, run_out = lax.fori_loop(
            0,
            tiles,
            step,
            (
                jnp.full((1, BLOCK), NEGATIVE, jnp.float32),
                jnp.zeros((1, BLOCK), jnp.float32),
                jnp.zeros((HDIM, BLOCK), jnp.float32),
            ),
        )
        attended = (run_out / run_sum).T
        out[rows, :] = attended
        out_low[rows, :] = attended.astype(jnp.bfloat16)
        top[i] = jnp.broadcast_to(new_top * rate + jnp.log2(run_sum), (8, BLOCK))


def attend_back_kernel(
    inverse, first, own, stop, q, k, v, out, top, d_out, dq, dk, dv, k_packed, k_turned, v_packed, k_sum, v_sum
):
    blocks = inverse.shape[0]
    scale = HDIM**-0.5
    rate = scale * LOG2E

    @pl.loop(0, blocks)
    def _(b):
        here = pl.ds(pl.multiple_of(b * BLOCK, BLOCK), BLOCK)
        there = pl.ds(pl.multiple_of(inverse[b] * BLOCK, BLOCK), BLOCK)
        k_packed[here, :] = k[there, :]
        k_turned[:, here] = k[there, :].T
        v_packed[here, :] = v[there, :]
        k_sum[here, :] = jnp.zeros((BLOCK, HDIM), jnp.float32)
        v_sum[here, :] = jnp.zeros((BLOCK, HDIM), jnp.float32)

    k_packed[blocks * BLOCK :, :] = jnp.zeros((TILE, HDIM), jnp.bfloat16)
    k_turned[:, blocks * BLOCK :] = jnp.zeros((HDIM, TILE), jnp.bfloat16)
    v_packed[blocks * BLOCK :, :] = jnp.zeros((TILE, HDIM), jnp.bfloat16)
    k_sum[blocks * BLOCK :, :] = jnp.zeros((TILE, HDIM), jnp.float32)
    v_sum[blocks * BLOCK :, :] = jnp.zeros((TILE, HDIM), jnp.float32)
    lane = lax.broadcasted_iota(jnp.int32, (1, BLOCK), 1)
    row = lax.broadcasted_iota(jnp.int32, (TILE, BLOCK), 0)

    @pl.loop(0, own.shape[0])
    def _(i):
        rows = pl.ds(pl.multiple_of(i * BLOCK, BLOCK), BLOCK)
        queries = q[rows, :]
        incoming = d_out[rows, :]
        shift = lax.dot_general(
            jnp.ones((8, HDIM), jnp.float32),
            incoming.astype(jnp.float32) * out[rows, :],
            (((1,), (1,)), ((), ())),
            precision=lax.Precision.HIGHEST,
            preferred_element_type=jnp.float32,
        )[0:1]
        level = top[i][0:1]
        start = first[i]
        limit = jnp.minimum(own[i] * BLOCK + lane, stop[i] - 1)
        tiles = (own[i] - start) // (TILE // BLOCK) + 1

        def step(t, grad):
            base = pl.multiple_of((start * BLOCK) + t * TILE, BLOCK)
            keys = pl.ds(base, TILE)
            found = across_rows(k_packed[keys, :], queries)
            weights = jnp.where(row <= limit - base, jnp.exp2(found * rate - level), 0.0)
            dots = across_rows(v_packed[keys, :], incoming)
            low_grad = (weights * ((dots - shift) * scale)).astype(jnp.bfloat16)
            v_sum[keys, :] += jnp.dot(
                weights.astype(jnp.bfloat16), incoming, preferred_element_type=jnp.float32
            )
            k_sum[keys, :] += jnp.dot(low_grad, queries, preferred_element_type=jnp.float32)
            return grad + jnp.dot(
                k_turned[:, keys], low_grad, preferred_element_type=jnp.float32
            )

        grad = lax.fori_loop(0, tiles, step, jnp.zeros((HDIM, BLOCK), jnp.float32))
        dq[rows, :] = grad.T.astype(jnp.bfloat16)

    @pl.loop(0, blocks)
    def _(b):
        here = pl.ds(pl.multiple_of(b * BLOCK, BLOCK), BLOCK)
        there = pl.ds(pl.multiple_of(inverse[b] * BLOCK, BLOCK), BLOCK)
        dk[there, :] = k_sum[here, :].astype(jnp.bfloat16)
        dv[there, :] = v_sum[here, :].astype(jnp.bfloat16)


def attend_calls(tables, q, k, v):
    smem = pl.BlockSpec(memory_space=pltpu.SMEM)
    vmem = pl.BlockSpec(memory_space=pltpu.VMEM)
    rows, all_rows = q.shape[0], k.shape[0]
    shape = jax.ShapeDtypeStruct
    f32, low = jnp.float32, jnp.bfloat16
    params = pltpu.CompilerParams(vmem_limit_bytes=60 << 20)
    wide = pltpu.VMEM((HDIM, all_rows + TILE), low)
    tall = pltpu.VMEM((all_rows + TILE, HDIM), low)
    tall_sum = pltpu.VMEM((all_rows + TILE, HDIM), f32)
    out, out_low, top = pl.pallas_call(
        attend_kernel,
        out_shape=[
            shape((rows, HDIM), f32),
            shape((rows, HDIM), low),
            shape((rows // BLOCK, 8, BLOCK), f32),
        ],
        in_specs=[smem] * 4 + [vmem] * 3,
        out_specs=[vmem] * 3,
        scratch_shapes=[tall, wide],
        compiler_params=params,
        name="attend",
    )(*tables, q, k, v)

    def back(d_out):
        return pl.pallas_call(
            attend_back_kernel,
            out_shape=[shape((rows, HDIM), low), shape((all_rows, HDIM), low), shape((all_rows, HDIM), low)],
            in_specs=[smem] * 4 + [vmem] * 6,
            out_specs=[vmem] * 3,
            scratch_shapes=[tall, wide, tall, tall_sum, tall_sum],
            compiler_params=params,
            name="attend_back",
        )(*tables, q, k, v, out, top, d_out)

    return out_low, back


def block_tables(seq_blocks, block_place, keep_all, line_rows, heads, count):
    total = block_place.shape[0]
    per = total // count
    seq_ends = jnp.cumsum(seq_blocks)
    seq_firsts = seq_ends - seq_blocks
    numbers = jnp.arange(total, dtype=jnp.int32)
    inverse = jnp.sum(
        jnp.where(block_place[None, :] == numbers[:, None], numbers[None, :], 0), axis=1
    )
    seq_of = jnp.sum((block_place[:, None] >= seq_ends[None, :]).astype(jnp.int32), axis=1)
    is_seq = seq_of[:, None] == jnp.arange(seq_blocks.shape[0], dtype=jnp.int32)[None, :]
    kept_blocks = jnp.sum(keep_all.reshape(total, BLOCK).astype(jnp.int32), axis=1)
    kept = jnp.sum(jnp.where(is_seq, kept_blocks[:, None], 0), axis=0)
    stop_of = seq_firsts * BLOCK + kept
    table = jnp.stack(
        [
            jnp.sum(jnp.where(is_seq, seq_firsts[None, :], 0), axis=1),
            block_place,
            jnp.sum(jnp.where(is_seq, stop_of[None, :], 0), axis=1),
        ]
    ).reshape(3, heads, count // heads, per)
    w = lax.rem(lax.axis_index("dp"), count // heads)
    mine = lax.dynamic_slice_in_dim(table, w, 1, 2).reshape(3, heads * per)
    return inverse, mine[0], mine[1], mine[2]


def row_scale(values):
    return lax.rsqrt(jnp.mean(values * values, axis=-1, keepdims=True) + EPSILON)


def rotate(values, positions):
    half_dim = values.shape[-1] // 2
    inv_freq = ROPE_BASE ** (-(jnp.arange(half_dim, dtype=jnp.float32) * 2.0) / values.shape[-1])
    turn_angle = positions.astype(jnp.float32)[:, None] * inv_freq[None, :]
    cosine = jnp.cos(turn_angle)[:, None, :]
    sine_vals = jnp.sin(turn_angle)[:, None, :]
    first_half = values[..., :half_dim]
    second_half = values[..., half_dim:]
    return jnp.concatenate(
        [
            first_half * cosine - second_half * sine_vals,
            second_half * cosine + first_half * sine_vals,
        ],
        axis=-1,
    )


def token_tables(seq_blocks, block_place, row_ids):
    block_total = block_place.shape[0]
    seq_total = seq_blocks.shape[0]
    seq_ends = jnp.cumsum(seq_blocks)
    seq_firsts = seq_ends - seq_blocks
    given_block = row_ids // BLOCK
    packed = jnp.sum(
        jnp.where(
            given_block[:, None] == jnp.arange(block_total, dtype=jnp.int32)[None, :],
            block_place[None, :],
            0,
        ),
        axis=1,
    )
    seq_of = jnp.sum((packed[:, None] >= seq_ends[None, :]).astype(jnp.int32), axis=1)
    first_of = jnp.sum(
        jnp.where(
            seq_of[:, None] == jnp.arange(seq_total, dtype=jnp.int32)[None, :],
            seq_firsts[None, :],
            0,
        ),
        axis=1,
    )
    return (seq_of, (packed - first_of) * BLOCK + row_ids % BLOCK)


def norm_back(values, row_factor, gain_row, incoming, model_width):
    scaled = gain_row * incoming
    inner_sum = jnp.sum(scaled * values, axis=-1, keepdims=True)
    return row_factor * scaled - values * (row_factor**3 / model_width) * inner_sum


def body(
    tokens,
    seq_blocks,
    block_place,
    pad_mask,
    expert_ids,
    attn_gain,
    w_qkv,
    qk_gain,
    w_out,
    ffn_gain,
    router,
    expert_in,
    expert_out,
    cotangent,
):
    rows_here = tokens.shape[0]
    model_width = tokens.shape[1]
    local_width = w_qkv.shape[2]
    heads_here = local_width // HDIM
    local_ff = expert_out.shape[1]
    tensor_index = lax.axis_index("tensor")
    feature_start = tensor_index * local_width
    first_row = lax.axis_index("dp") * rows_here
    row_ids = first_row + jnp.arange(rows_here, dtype=jnp.int32)
    seg_q, pos_q = token_tables(seq_blocks, block_place, row_ids)
    inputs = tokens.astype(jnp.float32)
    x_scale = row_scale(inputs)
    normed_in = (inputs * x_scale * attn_gain).astype(jnp.bfloat16)
    projected = jnp.dot(
        normed_in, w_qkv.reshape(model_width, 3 * local_width), preferred_element_type=jnp.float32
    ).reshape(rows_here, 3, local_width)
    queries = projected[:, 0]
    keys_here = projected[:, 1]
    values_here = projected[:, 2]
    sums_q, sums_k = lax.psum(
        (jnp.sum(queries * queries, axis=-1), jnp.sum(keys_here * keys_here, axis=-1)), "tensor"
    )
    q_scale = lax.rsqrt(sums_q / model_width + EPSILON)[:, None]
    k_scale = lax.rsqrt(sums_k / model_width + EPSILON)[:, None]
    q_norm = (queries * q_scale * qk_gain[0]).reshape(rows_here, heads_here, HDIM)
    k_norm = (keys_here * k_scale * qk_gain[1]).reshape(rows_here, heads_here, HDIM)
    q_rot = rotate(q_norm, pos_q).astype(jnp.bfloat16)
    k_rot = rotate(k_norm, pos_q).astype(jnp.bfloat16)
    v_low = values_here.astype(jnp.bfloat16)
    keep_here = pad_mask.astype(jnp.bfloat16)
    dp_count = lax.axis_size("dp")
    q_line, k_all, v_all, keep_all = spread_heads(
        q_rot.reshape(rows_here, local_width),
        k_rot.reshape(rows_here, local_width),
        v_low,
        jnp.broadcast_to(keep_here[None], (8, rows_here)),
        dp_count,
        heads_here,
        1,
    )
    tables = block_tables(
        seq_blocks, block_place, keep_all[:, 0], rows_here, heads_here, dp_count
    )
    total_rows = dp_count * rows_here
    line_out, attend_back = attend_calls(
        tables,
        q_line.reshape(heads_here * rows_here, HDIM),
        k_all.reshape(total_rows, HDIM),
        v_all.reshape(total_rows, HDIM),
    )
    attended_low = swap_line(
        line_out.reshape(heads_here, rows_here, HDIM), dp_count, heads_here, True, 2
    )
    branch = lax.psum(
        jnp.dot(attended_low, w_out, preferred_element_type=jnp.float32).astype(jnp.bfloat16),
        "tensor",
    ).astype(jnp.float32)
    hidden = inputs + branch
    h_scale = row_scale(hidden)
    normed = (hidden * h_scale * ffn_gain).astype(jnp.bfloat16)
    logits = jnp.dot(normed, router, preferred_element_type=jnp.float32)
    router_probs = jax.nn.softmax(logits, axis=-1)
    window_ids = jnp.arange(WIN, dtype=jnp.int32)
    chosen = jnp.any(expert_ids[:, :, None] == window_ids[None, None, :], axis=1)
    chosen_float = chosen.astype(jnp.float32)
    gate_values = router_probs[:, :WIN] * chosen_float
    slot_ids = jnp.arange(CAP, dtype=jnp.int32)
    token_ids = jnp.arange(rows_here, dtype=jnp.int32)
    mixture = jnp.zeros((rows_here, model_width), jnp.float32)
    saved_slots = []
    for expert in range(WIN):
        picked = chosen[:, expert]
        slot_rank = jnp.cumsum(picked.astype(jnp.int32)) - 1
        slot_table = (slot_rank[None, :] == slot_ids[:, None]) & picked[None, :]
        slot_token = jnp.sum(jnp.where(slot_table, token_ids[None, :], 0), axis=1)
        slot_live = jnp.any(slot_table, axis=1).astype(jnp.float32)
        gathered_rows = jnp.take(normed, slot_token, axis=0)
        gate_up = jnp.dot(
            gathered_rows,
            expert_in[expert].reshape(model_width, 2 * local_ff),
            preferred_element_type=jnp.float32,
        ).reshape(CAP, 2, local_ff)
        active = (jax.nn.silu(gate_up[:, 0]) * gate_up[:, 1]).astype(jnp.bfloat16)
        expert_part = jnp.dot(active, expert_out[expert], preferred_element_type=jnp.float32)
        slot_gate = jnp.take(gate_values[:, expert], slot_token) * slot_live
        mixture = mixture.at[slot_token].add(slot_gate[:, None] * expert_part)
        saved_slots.append(
            (slot_token, slot_live, gathered_rows, gate_up, active, expert_part, slot_gate)
        )
    mixture_share = lax.psum_scatter(
        mixture.astype(jnp.bfloat16), "tensor", scatter_dimension=1, tiled=True
    ).astype(jnp.float32)
    hidden_share = lax.dynamic_slice_in_dim(hidden, feature_start, local_width, 1)
    output = (hidden_share + mixture_share).astype(jnp.bfloat16)
    cot_full = lax.all_gather(cotangent, "tensor", axis=1, tiled=True).astype(jnp.float32)
    mixture_grad = jnp.zeros((rows_here, model_width), jnp.float32)
    gate_columns = []
    expert_in_list = []
    expert_out_list = []
    for expert in range(WIN):
        slot_token, slot_live, gathered_rows, gate_up, active, expert_part, slot_gate = saved_slots[
            expert
        ]
        cot_rows = jnp.take(cot_full, slot_token, axis=0)
        part_grad = (slot_gate[:, None] * cot_rows).astype(jnp.bfloat16)
        slot_dots = jnp.sum(cot_rows * expert_part, axis=-1) * slot_live
        gate_columns.append(jnp.zeros((rows_here,), jnp.float32).at[slot_token].add(slot_dots))
        expert_out_list.append(
            jnp.einsum("cf,cd->fd", active, part_grad, preferred_element_type=jnp.float32)
        )
        active_grad = jnp.einsum(
            "cd,fd->cf", part_grad, expert_out[expert], preferred_element_type=jnp.float32
        )
        _, silu_pull = jax.vjp(
            lambda gate_in, up_in: jax.nn.silu(gate_in) * up_in, gate_up[:, 0], gate_up[:, 1]
        )
        gate_in_grad, up_in_grad = silu_pull(active_grad)
        pair_grad = (
            jnp.stack([gate_in_grad, up_in_grad], axis=1)
            .astype(jnp.bfloat16)
            .reshape(CAP, 2 * local_ff)
        )
        expert_in_list.append(
            jnp.einsum(
                "cd,cf->df", gathered_rows, pair_grad, preferred_element_type=jnp.float32
            ).reshape(model_width, 2, local_ff)
        )
        row_grad = jnp.einsum(
            "cf,df->cd",
            pair_grad,
            expert_in[expert].reshape(model_width, 2 * local_ff),
            preferred_element_type=jnp.float32,
        )
        mixture_grad = mixture_grad.at[slot_token].add(row_grad)
    gate_grad = jnp.stack(gate_columns, axis=1)
    mixture_grad, gate_grad = (
        lax.psum(mixture_grad.astype(jnp.bfloat16), "tensor").astype(jnp.float32),
        lax.psum(gate_grad.astype(jnp.bfloat16), "tensor").astype(jnp.float32),
    )
    probs_grad = jnp.concatenate(
        [gate_grad * chosen_float, jnp.zeros((rows_here, router.shape[1] - WIN), jnp.float32)],
        axis=1,
    )
    logit_grad = (
        router_probs * (probs_grad - jnp.sum(router_probs * probs_grad, axis=-1, keepdims=True))
    ).astype(jnp.bfloat16)
    normed_grad = mixture_grad + jnp.einsum(
        "te,de->td", logit_grad, router, preferred_element_type=jnp.float32
    )
    normed_share = lax.dynamic_slice_in_dim(normed, feature_start, local_width, 1)
    router_grad = jnp.einsum(
        "td,te->de", normed_share, logit_grad, preferred_element_type=jnp.float32
    )
    ffn_gain_grad = lax.dynamic_slice_in_dim(
        jnp.sum(normed_grad * hidden * h_scale, axis=0), feature_start, local_width, 0
    )
    hidden_grad = cot_full + norm_back(hidden, h_scale, ffn_gain, normed_grad, model_width)
    expert_in_grad = jnp.stack(expert_in_list)
    expert_out_grad = jnp.stack(expert_out_list)
    branch_grad = hidden_grad.astype(jnp.bfloat16)
    out_grad = jnp.einsum(
        "tc,td->cd", attended_low, branch_grad, preferred_element_type=jnp.float32
    )
    attended_grad = jnp.einsum(
        "td,cd->tc", branch_grad, w_out, preferred_element_type=jnp.float32
    ).astype(jnp.bfloat16)
    line_grad = swap_line(attended_grad, dp_count, heads_here, False, 3)
    dq_line, dk_line, dv_line = attend_back(line_grad.reshape(heads_here * rows_here, HDIM))
    query_grad, key_grad, value_low_grad = return_heads(
        dq_line.reshape(heads_here, rows_here, HDIM),
        dk_line.reshape(dp_count, rows_here, HDIM),
        dv_line.reshape(dp_count, rows_here, HDIM),
        dp_count,
        heads_here,
        4,
    )
    query_grad = query_grad.astype(jnp.float32).reshape(rows_here, heads_here, HDIM)
    key_grad = key_grad.astype(jnp.float32)
    _, rope_pull = jax.vjp(lambda turned: rotate(turned, pos_q), q_norm)
    q_norm_grad = rope_pull(query_grad)[0].reshape(rows_here, local_width)
    k_norm_grad = rope_pull(key_grad.reshape(rows_here, heads_here, HDIM))[0].reshape(
        rows_here, local_width
    )
    scaled_q = qk_gain[0] * q_norm_grad
    scaled_k = qk_gain[1] * k_norm_grad
    inner_q, inner_k = lax.psum(
        (jnp.sum(scaled_q * queries, axis=-1), jnp.sum(scaled_k * keys_here, axis=-1)), "tensor"
    )
    q_grad = (
        q_scale * scaled_q - queries * (q_scale**3 / model_width) * inner_q[:, None]
    ).astype(jnp.bfloat16)
    k_grad = (
        k_scale * scaled_k - keys_here * (k_scale**3 / model_width) * inner_k[:, None]
    ).astype(jnp.bfloat16)
    qk_gain_grad = jnp.stack(
        [
            jnp.sum(q_norm_grad * queries * q_scale, axis=0),
            jnp.sum(k_norm_grad * keys_here * k_scale, axis=0),
        ]
    )
    proj_grad = jnp.stack([q_grad, k_grad, value_low_grad], axis=1).reshape(
        rows_here, 3 * local_width
    )
    qkv_grad = jnp.einsum(
        "td,tc->dc", normed_in, proj_grad, preferred_element_type=jnp.float32
    ).reshape(model_width, 3, local_width)
    normed_in_grad = jnp.einsum(
        "tc,dc->td",
        proj_grad,
        w_qkv.reshape(model_width, 3 * local_width),
        preferred_element_type=jnp.float32,
    )
    input_part = norm_back(inputs, x_scale, attn_gain, normed_in_grad, model_width)
    gain_part = jnp.sum(normed_in_grad * inputs * x_scale, axis=0)
    input_sum, attn_gain_grad = (
        lax.psum_scatter(
            input_part.astype(jnp.bfloat16), "tensor", scatter_dimension=1, tiled=True
        ).astype(jnp.float32),
        lax.psum_scatter(
            gain_part.astype(jnp.bfloat16), "tensor", scatter_dimension=0, tiled=True
        ).astype(jnp.float32),
    )
    input_grad = (
        lax.dynamic_slice_in_dim(hidden_grad, feature_start, local_width, 1) + input_sum
    ).astype(jnp.bfloat16)
    small = jnp.concatenate(
        [
            router_grad.reshape(-1, 256),
            jnp.concatenate([attn_gain_grad, ffn_gain_grad, qk_gain_grad.reshape(-1)]).reshape(
                -1, 256
            ),
        ]
    ).astype(jnp.bfloat16)
    small_rows = small.shape[0]
    small = jnp.pad(small, ((0, -small_rows % (dp_count * 8)), (0, 0)))
    low = jnp.bfloat16
    qkv_sum, out_sum, in_sum, exp_sum, small_sum = ring_sum(
        [
            jnp.transpose(qkv_grad, (1, 0, 2)).astype(low),
            out_grad.astype(low)[None],
            expert_in_grad.reshape(WIN, model_width, 2 * local_ff).astype(low),
            expert_out_grad.astype(low),
            small[None],
        ],
        dp_count,
        0,
    )
    qkv_grad = jnp.transpose(qkv_sum.astype(jnp.float32), (1, 0, 2))
    out_grad = out_sum[0].astype(jnp.float32)
    expert_in_grad = in_sum.astype(jnp.float32).reshape(expert_in_grad.shape)
    expert_out_grad = exp_sum.astype(jnp.float32)
    router_rows = router_grad.size // 256
    small_sum = small_sum[0].astype(jnp.float32)
    router_grad = small_sum[:router_rows].reshape(router_grad.shape)
    gains = small_sum[router_rows:small_rows].reshape(-1)
    attn_gain_grad = gains[:local_width]
    ffn_gain_grad = gains[local_width : 2 * local_width]
    qk_gain_grad = gains[2 * local_width :].reshape(2, local_width)
    return (
        output,
        input_grad,
        attn_gain_grad,
        qkv_grad,
        qk_gain_grad,
        out_grad,
        ffn_gain_grad,
        router_grad,
        expert_in_grad,
        expert_out_grad,
    )


def solution(mesh):
    placed = (
        P("dp", None),
        P(),
        P(),
        P("dp"),
        P("dp", None),
        P(),
        P(None, None, "tensor"),
        P(None, "tensor"),
        P("tensor", None),
        P(),
        P(),
        P(None, None, None, "tensor"),
        P(None, "tensor", None),
        P("dp", "tensor"),
    )
    return jax.shard_map(
        body,
        mesh=mesh,
        in_specs=placed,
        out_specs=(
            P("dp", "tensor"),
            P("dp", "tensor"),
            P("tensor"),
            P(None, None, "tensor"),
            P(None, "tensor"),
            P("tensor", None),
            P("tensor"),
            P("tensor", None),
            P(None, None, None, "tensor"),
            P(None, "tensor", None),
        ),
        check_vma=False,
    )
```

```python
import functools

import jax
import jax.numpy as jnp
from jax import lax
from jax.experimental import pallas as pl
from jax.experimental.pallas import tpu as pltpu
from jax.sharding import PartitionSpec as P

MESH = pl.DeviceIdType.MESH

HDIM = 128
WIN = 2
BLOCK = 128
CAP = 128


EPSILON = 1e-05
ROPE_BASE = 10000.0
NEGATIVE = -1e30
LOG2E = 1.4426950408889634
TILE = 512


def ring_place(index, count):
    if count != 8:
        return index
    z, y = index // 2, index % 2
    return z + y * (7 - 2 * z)


def ring_index(place, count):
    place = lax.rem(place + 2 * count, count)
    if count != 8:
        return place
    y = place // 4
    z = place - y * (2 * place - 7)
    return z * 2 + y


def ring_kernel(count, parts, *refs):
    ins, outs, slots = refs[:parts], refs[parts : 2 * parts], refs[2 * parts : 3 * parts]
    send_sem, recv_sem = refs[3 * parts :]
    me = ring_place(lax.axis_index("dp"), count)
    tensor = lax.axis_index("tensor")
    ahead = (
        (ring_index(me + 1, count), tensor),
        (ring_index(me - 1, count), tensor),
    )
    barrier = pltpu.get_barrier_semaphore()
    for device in ahead:
        pl.semaphore_signal(barrier, inc=1, device_id=device, device_id_type=MESH)
    pl.semaphore_wait(barrier, 2)

    def block(part, way, number):
        rows = ins[part].shape[1] // count
        half = ins[part].shape[2] // 2
        number = lax.rem(number + 2 * count, count)
        start = pl.multiple_of(number * rows, rows)
        return (slice(None), pl.ds(start, rows), pl.ds(way * half, half))

    def scatter_copy(part, way, step, source):
        return pltpu.make_async_remote_copy(
            src_ref=source,
            dst_ref=slots[part].at[way, step],
            send_sem=send_sem.at[0, way, step, part],
            recv_sem=recv_sem.at[0, way, step, part],
            device_id=ahead[way],
            device_id_type=MESH,
        )

    def gather_copy(part, way, step, number):
        where = outs[part].at[block(part, way, number)]
        return pltpu.make_async_remote_copy(
            src_ref=where,
            dst_ref=where,
            send_sem=send_sem.at[1, way, step, part],
            recv_sem=recv_sem.at[1, way, step, part],
            device_id=ahead[way],
            device_id_type=MESH,
        )

    both = [(part, way) for part in range(parts) for way in (0, 1)]
    sign = (1, -1)
    for part, way in both:
        scatter_copy(part, way, 0, ins[part].at[block(part, way, me)]).start()

    def add_own(part, way, step, target):
        where = block(part, way, me - sign[way] * (step + 1))
        depth, rows = ins[part].shape[0], ins[part].shape[1] // count
        piece = min(rows, 32)
        for layer in range(depth):

            @pl.loop(0, rows // piece)
            def _(turn):
                here = pl.ds(pl.multiple_of(turn * piece, piece), piece)
                mine = ins[part].at[where].at[layer, here, :]
                came = slots[part].at[way, step, layer, here, :]
                total = mine[...].astype(jnp.float32) + came[...].astype(jnp.float32)
                target.at[layer, here, :][...] = total.astype(jnp.bfloat16)

    @pl.loop(0, count - 2)
    def _(step):
        for part, way in both:
            source = slots[part].at[way, step]
            scatter_copy(part, way, step, source).wait_recv()
            add_own(part, way, step, source)
            scatter_copy(part, way, step + 1, source).start()

    last = count - 2
    for part, way in both:
        scatter_copy(part, way, last, slots[part].at[way, last]).wait_recv()
        mine = me + sign[way]
        add_own(part, way, last, outs[part].at[block(part, way, mine)])
        gather_copy(part, way, 0, mine).start()

    @pl.loop(0, count - 2)
    def _(step):
        for part, way in both:
            number = me - sign[way] * step
            gather_copy(part, way, step, number).wait_recv()
            gather_copy(part, way, step + 1, number).start()

    for part, way in both:
        gather_copy(part, way, last, me - sign[way] * last).wait_recv()

    @pl.loop(0, count - 1)
    def _(step):
        for part, way in both:
            scatter_copy(part, way, step, slots[part].at[way, step]).wait_send()
            gather_copy(part, way, step, me + sign[way] * (1 - step)).wait_send()


def ring_sum(arrays, count, number):
    parts = len(arrays)
    slots = [
        pltpu.VMEM((2, count - 1, a.shape[0], a.shape[1] // count, a.shape[2] // 2), jnp.bfloat16)
        for a in arrays
    ]
    sems = pltpu.SemaphoreType.DMA((2, 2, count - 1, parts))
    return pl.pallas_call(
        functools.partial(ring_kernel, count, parts),
        out_shape=[jax.ShapeDtypeStruct(a.shape, jnp.bfloat16) for a in arrays],
        in_specs=[pl.BlockSpec(memory_space=pltpu.VMEM)] * parts,
        out_specs=[pl.BlockSpec(memory_space=pltpu.VMEM)] * parts,
        scratch_shapes=[*slots, sems, sems],
        compiler_params=pltpu.CompilerParams(
            collective_id=number, has_side_effects=True, vmem_limit_bytes=60 << 20
        ),
        name="ring_sum",
    )(*arrays)


def line_place(count, heads):
    me = lax.axis_index("dp")
    across = count // heads
    return me // across, lax.rem(me, across), across


def greet(devices):
    barrier = pltpu.get_barrier_semaphore()
    for device in devices:
        pl.semaphore_signal(barrier, inc=1, device_id=device, device_id_type=MESH)
    pl.semaphore_wait(barrier, len(devices))


def line_devices(count, heads):
    z, w, across = line_place(count, heads)
    tensor = lax.axis_index("tensor")
    along = [(lax.rem(z + dz, heads) * across + w, tensor) for dz in range(1, heads)]
    beside = [(z * across + lax.rem(w + dw, across), tensor) for dw in range(1, across)]
    return along, beside


def head_columns(number):
    return (slice(None), pl.ds(pl.multiple_of(number * HDIM, HDIM), HDIM))


def spread_kernel(
    count, heads, q, k, v, keep, cot, w_in, q_all, k_all, v_all, keep_all, cot_all, w_split, *sems
):
    send_one, recv_one, send_two, recv_two, near, send_cot, recv_cot = sems
    dp, t = lax.axis_index("dp"), lax.axis_index("tensor")
    _, _, beside_core, cross, last = tensor_partners()
    z, w, across = line_place(count, heads)
    me = z * across + w
    along, beside = line_devices(count, heads)
    greet(along + beside + [(dp, beside_core), (dp, cross)])
    pairs = ((k, k_all), (v, v_all), (keep, keep_all), (q, q_all))

    def piece(item, head):
        source = pairs[item][0]
        return source if item == 2 else source.at[head_columns(head)]

    def first_copy(item, dz):
        head = lax.rem(z + dz, heads)
        return pltpu.make_async_remote_copy(
            src_ref=piece(item, head),
            dst_ref=pairs[item][1].at[z if item == 3 else me],
            send_sem=send_one.at[item, dz - 1],
            recv_sem=recv_one.at[item, dz - 1],
            device_id=along[dz - 1],
            device_id_type=MESH,
        )

    def second_copy(item, dz, dw):
        where = lax.rem(z - dz + heads, heads) * across + w
        return pltpu.make_async_remote_copy(
            src_ref=piece(item, z) if dz == 0 else pairs[item][1].at[where],
            dst_ref=pairs[item][1].at[where],
            send_sem=send_two.at[item, dz, dw - 1],
            recv_sem=recv_two.at[item, dz, dw - 1],
            device_id=beside[dw - 1],
            device_id_type=MESH,
        )

    def columns_of(owner):
        width = cot.shape[1]
        return cot_all.at[:, pl.ds(pl.multiple_of(owner * width, width), width)]

    def cot_copy(place, owner):
        return pltpu.make_async_remote_copy(
            src_ref=columns_of(owner) if place == 2 else cot,
            dst_ref=columns_of(owner),
            send_sem=send_cot.at[place],
            recv_sem=recv_cot.at[place],
            device_id=(dp, cross if place == 1 else beside_core),
            device_id_type=MESH,
        )

    first = [(item, dz) for dz in range(1, heads) for item in range(4)]
    second = [(dz, item, dw) for dz in range(heads) for item in range(3) for dw in range(1, across)]
    local = []
    for item, dz in first:
        first_copy(item, dz).start()
    for dz, item, dw in second:
        if dz == 0:
            second_copy(item, dz, dw).start()
    for item in range(4):
        own = pairs[item][1].at[z if item == 3 else me]
        copy = pltpu.make_async_copy(piece(item, z), own, near.at[item])
        copy.start()
        local.append(copy)
    cot_copy(0, t).start()
    cot_copy(1, t).start()
    copy = pltpu.make_async_copy(cot, columns_of(t), near.at[4])
    copy.start()
    local.append(copy)

    @pl.loop(0, w_in.shape[0])
    def _(e):
        @pl.loop(0, w_in.shape[1] // 128)
        def _(turn):
            here = pl.ds(pl.multiple_of(turn * 128, 128), 128)
            w_split[e, 0, here, :] = w_in[e, here, 0, :]
            w_split[e, 1, here, :] = w_in[e, here, 1, :]

    cot_copy(1, cross).wait_recv()
    cot_copy(2, cross).start()
    for item, dz in first:
        first_copy(item, dz).wait_recv()
        if item < 3:
            for dw in range(1, across):
                second_copy(item, dz, dw).start()
    for dz, item, dw in second:
        second_copy(item, dz, dw).wait_recv()
    for item, dz in first:
        first_copy(item, dz).wait_send()
    for dz, item, dw in second:
        second_copy(item, dz, dw).wait_send()
    cot_copy(0, beside_core).wait_recv()
    cot_copy(2, last).wait_recv()
    for place in range(3):
        cot_copy(place, cross if place == 2 else t).wait_send()
    for copy in local:
        copy.wait()


def spread_heads(q, k, v, keep, cot, w_in, count, heads, number):
    rows = q.shape[0]
    across = count // heads
    sem = pltpu.SemaphoreType.DMA
    window, deep, _, units = w_in.shape
    shapes = [
        (heads, rows, HDIM),
        (count, rows, HDIM),
        (count, rows, HDIM),
        (count, *keep.shape),
        (rows, 4 * cot.shape[1]),
        (window, 2, deep, units),
    ]
    return pl.pallas_call(
        functools.partial(spread_kernel, count, heads),
        out_shape=[jax.ShapeDtypeStruct(shape, jnp.bfloat16) for shape in shapes],
        in_specs=[pl.BlockSpec(memory_space=pl.ANY)] * 5
        + [pl.BlockSpec(memory_space=pltpu.VMEM)],
        out_specs=[pl.BlockSpec(memory_space=pl.ANY)] * 5
        + [pl.BlockSpec(memory_space=pltpu.VMEM)],
        scratch_shapes=[
            sem((4, heads - 1)),
            sem((4, heads - 1)),
            sem((3, heads, across - 1)),
            sem((3, heads, across - 1)),
            sem((5,)),
            sem((3,)),
            sem((3,)),
        ],
        compiler_params=pltpu.CompilerParams(
            collective_id=number, has_side_effects=True, vmem_limit_bytes=40 << 20
        ),
        name="spread_heads",
    )(q, k, v, keep, cot, w_in)


def swap_kernel(count, heads, join, source, result, send_sem, recv_sem, near):
    z, w, across = line_place(count, heads)
    along, _ = line_devices(count, heads)
    greet(along)

    def copy_to(dz):
        far = lax.rem(z + dz, heads)
        return pltpu.make_async_remote_copy(
            src_ref=source.at[far] if join else source.at[head_columns(far)],
            dst_ref=result.at[head_columns(z)] if join else result.at[z],
            send_sem=send_sem.at[dz - 1],
            recv_sem=recv_sem.at[dz - 1],
            device_id=along[dz - 1],
            device_id_type=MESH,
        )

    for dz in range(1, heads):
        copy_to(dz).start()
    own = pltpu.make_async_copy(
        source.at[z] if join else source.at[head_columns(z)],
        result.at[head_columns(z)] if join else result.at[z],
        near,
    )
    own.start()
    for dz in range(1, heads):
        copy_to(dz).wait()
    own.wait()


def swap_line(source, count, heads, join, number):
    rows = source.shape[1] if join else source.shape[0]
    shape = (rows, heads * HDIM) if join else (heads, rows, HDIM)
    sem = pltpu.SemaphoreType.DMA
    return pl.pallas_call(
        functools.partial(swap_kernel, count, heads, join),
        out_shape=jax.ShapeDtypeStruct(shape, jnp.bfloat16),
        in_specs=[pl.BlockSpec(memory_space=pl.ANY)],
        out_specs=pl.BlockSpec(memory_space=pl.ANY),
        scratch_shapes=[sem((heads - 1,)), sem((heads - 1,)), sem],
        compiler_params=pltpu.CompilerParams(collective_id=number, has_side_effects=True),
        name="join_heads" if join else "part_heads",
    )(source)


def return_kernel(count, heads, dq, dk, dv, dq_own, dk_own, dv_own, came_k, came_v, total_k, total_v, *sems):
    send_one, recv_one, send_two, recv_two, near = sems
    z, w, across = line_place(count, heads)
    along, beside = line_devices(count, heads)
    greet(along + beside)
    partial = ((dk, came_k, total_k), (dv, came_v, total_v))
    whole = (dk_own, dv_own, dq_own)
    lines = [lax.rem(z + dz, heads) for dz in (*range(1, heads), 0)]

    def first_copy(item, turn, dw):
        return pltpu.make_async_remote_copy(
            src_ref=partial[item][0].at[lines[turn] * across + lax.rem(w + dw, across)],
            dst_ref=partial[item][1].at[turn, dw - 1],
            send_sem=send_one.at[item, turn, dw - 1],
            recv_sem=recv_one.at[item, turn, dw - 1],
            device_id=beside[dw - 1],
            device_id_type=MESH,
        )

    def second_copy(item, turn):
        return pltpu.make_async_remote_copy(
            src_ref=dq.at[lines[turn]] if item == 2 else partial[item][2].at[turn],
            dst_ref=whole[item].at[head_columns(z)],
            send_sem=send_two.at[item, turn],
            recv_sem=recv_two.at[item, turn],
            device_id=along[turn],
            device_id_type=MESH,
        )

    def landed(item, turn):
        back = lax.rem(z - turn - 1 + heads, heads)
        where = whole[item].at[head_columns(back)]
        return pltpu.make_async_remote_copy(
            src_ref=where,
            dst_ref=where,
            send_sem=send_two.at[item, turn],
            recv_sem=recv_two.at[item, turn],
            device_id=along[turn],
            device_id_type=MESH,
        )

    rows = dk.shape[1]
    piece = 128
    first = [(item, turn, dw) for turn in range(heads) for item in (0, 1) for dw in range(1, across)]
    for item, turn, dw in first:
        first_copy(item, turn, dw).start()
    for turn in range(heads - 1):
        second_copy(2, turn).start()
    local = [pltpu.make_async_copy(dq.at[z], dq_own.at[head_columns(z)], near.at[2])]
    local[0].start()
    for turn in range(heads):
        for item in (0, 1):
            own, came, total = partial[item]
            for dw in range(1, across):
                first_copy(item, turn, dw).wait_recv()

            @pl.loop(0, rows // piece)
            def _(part):
                here = pl.ds(pl.multiple_of(part * piece, piece), piece)
                result = own[lines[turn] * across + w, here, :].astype(jnp.float32)
                for dw in range(1, across):
                    result = result + came[turn, dw - 1, here, :].astype(jnp.float32)
                total[turn, here, :] = result.astype(jnp.bfloat16)

            if turn < heads - 1:
                second_copy(item, turn).start()
            else:
                copy = pltpu.make_async_copy(
                    total.at[turn], whole[item].at[head_columns(z)], near.at[item]
                )
                copy.start()
                local.append(copy)
    for item in range(3):
        for turn in range(heads - 1):
            landed(item, turn).wait_recv()
            second_copy(item, turn).wait_send()
    for item, turn, dw in first:
        first_copy(item, turn, dw).wait_send()
    for copy in local:
        copy.wait()


def return_heads(dq, dk, dv, count, heads, number):
    rows = dq.shape[1]
    across = count // heads
    sem = pltpu.SemaphoreType.DMA
    vmem = pl.BlockSpec(memory_space=pltpu.VMEM)
    came = pltpu.VMEM((heads, across - 1, rows, HDIM), jnp.bfloat16)
    total = pltpu.VMEM((heads, rows, HDIM), jnp.bfloat16)
    own = jax.ShapeDtypeStruct((rows, heads * HDIM), jnp.bfloat16)
    return pl.pallas_call(
        functools.partial(return_kernel, count, heads),
        out_shape=[own] * 3,
        in_specs=[vmem] * 3,
        out_specs=[vmem] * 3,
        scratch_shapes=[
            came,
            came,
            total,
            total,
            sem((2, heads, across - 1)),
            sem((2, heads, across - 1)),
            sem((3, heads - 1)),
            sem((3, heads - 1)),
            sem((3,)),
        ],
        compiler_params=pltpu.CompilerParams(
            collective_id=number, has_side_effects=True, vmem_limit_bytes=60 << 20
        ),
        name="return_heads",
    )(dq, dk, dv)


def across_rows(left, right):
    return lax.dot_general(
        left, right, (((1,), (1,)), ((), ())), preferred_element_type=jnp.float32
    )


def attend_kernel(inverse, first, own, stop, q, k, v, out, out_low, top, k_packed, v_turned):
    blocks = inverse.shape[0]
    rate = HDIM**-0.5 * LOG2E

    @pl.loop(0, blocks)
    def _(b):
        here = pl.ds(pl.multiple_of(b * BLOCK, BLOCK), BLOCK)
        there = pl.ds(pl.multiple_of(inverse[b] * BLOCK, BLOCK), BLOCK)
        k_packed[here, :] = k[there, :]
        v_turned[:, here] = v[there, :].T

    k_packed[blocks * BLOCK :, :] = jnp.zeros((TILE, HDIM), jnp.bfloat16)
    v_turned[:, blocks * BLOCK :] = jnp.zeros((HDIM, TILE), jnp.bfloat16)
    lane = lax.broadcasted_iota(jnp.int32, (1, BLOCK), 1)
    row = lax.broadcasted_iota(jnp.int32, (TILE, BLOCK), 0)

    @pl.loop(0, own.shape[0])
    def _(i):
        rows = pl.ds(pl.multiple_of(i * BLOCK, BLOCK), BLOCK)
        queries = q[rows, :]
        start = first[i]
        limit = jnp.minimum(own[i] * BLOCK + lane, stop[i] - 1)
        tiles = (own[i] - start) // (TILE // BLOCK) + 1

        def step(t, state):
            run_top, run_sum, run_out = state
            base = pl.multiple_of((start * BLOCK) + t * TILE, BLOCK)
            keys = pl.ds(base, TILE)
            found = across_rows(k_packed[keys, :], queries)
            found = jnp.where(row <= limit - base, found, NEGATIVE)
            new_top = jnp.maximum(run_top, jnp.max(found, axis=0, keepdims=True))
            factor = jnp.exp2((run_top - new_top) * rate)
            weights = jnp.exp2((found - new_top) * rate)
            run_sum = run_sum * factor + jnp.sum(weights, axis=0, keepdims=True)
            run_out = run_out * factor + jnp.dot(
                v_turned[:, keys],
                weights.astype(jnp.bfloat16),
                preferred_element_type=jnp.float32,
            )
            return new_top, run_sum, run_out

        new_top, run_sum, run_out = lax.fori_loop(
            0,
            tiles,
            step,
            (
                jnp.full((1, BLOCK), NEGATIVE, jnp.float32),
                jnp.zeros((1, BLOCK), jnp.float32),
                jnp.zeros((HDIM, BLOCK), jnp.float32),
            ),
        )
        attended = (run_out / run_sum).T
        out[rows, :] = attended
        out_low[rows, :] = attended.astype(jnp.bfloat16)
        top[i] = jnp.broadcast_to(new_top * rate + jnp.log2(run_sum), (8, BLOCK))


def attend_back_kernel(
    inverse, first, own, stop, q, k, v, out, top, d_out, dq, dk, dv, k_packed, k_turned, v_packed, k_sum, v_sum
):
    blocks = inverse.shape[0]
    scale = HDIM**-0.5
    rate = scale * LOG2E

    @pl.loop(0, blocks)
    def _(b):
        here = pl.ds(pl.multiple_of(b * BLOCK, BLOCK), BLOCK)
        there = pl.ds(pl.multiple_of(inverse[b] * BLOCK, BLOCK), BLOCK)
        k_packed[here, :] = k[there, :]
        k_turned[:, here] = k[there, :].T
        v_packed[here, :] = v[there, :]
        k_sum[here, :] = jnp.zeros((BLOCK, HDIM), jnp.float32)
        v_sum[here, :] = jnp.zeros((BLOCK, HDIM), jnp.float32)

    k_packed[blocks * BLOCK :, :] = jnp.zeros((TILE, HDIM), jnp.bfloat16)
    k_turned[:, blocks * BLOCK :] = jnp.zeros((HDIM, TILE), jnp.bfloat16)
    v_packed[blocks * BLOCK :, :] = jnp.zeros((TILE, HDIM), jnp.bfloat16)
    k_sum[blocks * BLOCK :, :] = jnp.zeros((TILE, HDIM), jnp.float32)
    v_sum[blocks * BLOCK :, :] = jnp.zeros((TILE, HDIM), jnp.float32)
    lane = lax.broadcasted_iota(jnp.int32, (1, BLOCK), 1)
    row = lax.broadcasted_iota(jnp.int32, (TILE, BLOCK), 0)

    @pl.loop(0, own.shape[0])
    def _(i):
        rows = pl.ds(pl.multiple_of(i * BLOCK, BLOCK), BLOCK)
        queries = q[rows, :]
        incoming = d_out[rows, :]
        shift = lax.dot_general(
            jnp.ones((8, HDIM), jnp.float32),
            incoming.astype(jnp.float32) * out[rows, :],
            (((1,), (1,)), ((), ())),
            precision=lax.Precision.HIGHEST,
            preferred_element_type=jnp.float32,
        )[0:1]
        level = top[i][0:1]
        start = first[i]
        limit = jnp.minimum(own[i] * BLOCK + lane, stop[i] - 1)
        tiles = (own[i] - start) // (TILE // BLOCK) + 1

        def step(t, grad):
            base = pl.multiple_of((start * BLOCK) + t * TILE, BLOCK)
            keys = pl.ds(base, TILE)
            found = across_rows(k_packed[keys, :], queries)
            weights = jnp.where(row <= limit - base, jnp.exp2(found * rate - level), 0.0)
            dots = across_rows(v_packed[keys, :], incoming)
            low_grad = (weights * ((dots - shift) * scale)).astype(jnp.bfloat16)
            v_sum[keys, :] += jnp.dot(
                weights.astype(jnp.bfloat16), incoming, preferred_element_type=jnp.float32
            )
            k_sum[keys, :] += jnp.dot(low_grad, queries, preferred_element_type=jnp.float32)
            return grad + jnp.dot(
                k_turned[:, keys], low_grad, preferred_element_type=jnp.float32
            )

        grad = lax.fori_loop(0, tiles, step, jnp.zeros((HDIM, BLOCK), jnp.float32))
        dq[rows, :] = grad.T.astype(jnp.bfloat16)

    @pl.loop(0, blocks)
    def _(b):
        here = pl.ds(pl.multiple_of(b * BLOCK, BLOCK), BLOCK)
        there = pl.ds(pl.multiple_of(inverse[b] * BLOCK, BLOCK), BLOCK)
        dk[there, :] = k_sum[here, :].astype(jnp.bfloat16)
        dv[there, :] = v_sum[here, :].astype(jnp.bfloat16)


def attend_calls(tables, q, k, v):
    smem = pl.BlockSpec(memory_space=pltpu.SMEM)
    vmem = pl.BlockSpec(memory_space=pltpu.VMEM)
    rows, all_rows = q.shape[0], k.shape[0]
    shape = jax.ShapeDtypeStruct
    f32, low = jnp.float32, jnp.bfloat16
    params = pltpu.CompilerParams(vmem_limit_bytes=60 << 20)
    wide = pltpu.VMEM((HDIM, all_rows + TILE), low)
    tall = pltpu.VMEM((all_rows + TILE, HDIM), low)
    tall_sum = pltpu.VMEM((all_rows + TILE, HDIM), f32)
    out, out_low, top = pl.pallas_call(
        attend_kernel,
        out_shape=[
            shape((rows, HDIM), f32),
            shape((rows, HDIM), low),
            shape((rows // BLOCK, 8, BLOCK), f32),
        ],
        in_specs=[smem] * 4 + [vmem] * 3,
        out_specs=[vmem] * 3,
        scratch_shapes=[tall, wide],
        compiler_params=params,
        name="attend",
    )(*tables, q, k, v)

    def back(d_out):
        return pl.pallas_call(
            attend_back_kernel,
            out_shape=[shape((rows, HDIM), low), shape((all_rows, HDIM), low), shape((all_rows, HDIM), low)],
            in_specs=[smem] * 4 + [vmem] * 6,
            out_specs=[vmem] * 3,
            scratch_shapes=[tall, wide, tall, tall_sum, tall_sum],
            compiler_params=params,
            name="attend_back",
        )(*tables, q, k, v, out, top, d_out)

    return out_low, back


def block_tables(seq_blocks, block_place, keep_all, line_rows, heads, count):
    total = block_place.shape[0]
    per = total // count
    seq_ends = jnp.cumsum(seq_blocks)
    seq_firsts = seq_ends - seq_blocks
    numbers = jnp.arange(total, dtype=jnp.int32)
    inverse = jnp.sum(
        jnp.where(block_place[None, :] == numbers[:, None], numbers[None, :], 0), axis=1
    )
    seq_of = jnp.sum((block_place[:, None] >= seq_ends[None, :]).astype(jnp.int32), axis=1)
    is_seq = seq_of[:, None] == jnp.arange(seq_blocks.shape[0], dtype=jnp.int32)[None, :]
    kept_blocks = jnp.sum(keep_all.reshape(total, BLOCK).astype(jnp.int32), axis=1)
    kept = jnp.sum(jnp.where(is_seq, kept_blocks[:, None], 0), axis=0)
    stop_of = seq_firsts * BLOCK + kept
    table = jnp.stack(
        [
            jnp.sum(jnp.where(is_seq, seq_firsts[None, :], 0), axis=1),
            block_place,
            jnp.sum(jnp.where(is_seq, stop_of[None, :], 0), axis=1),
        ]
    ).reshape(3, heads, count // heads, per)
    w = lax.rem(lax.axis_index("dp"), count // heads)
    mine = lax.dynamic_slice_in_dim(table, w, 1, 2).reshape(3, heads * per)
    return inverse, mine[0], mine[1], mine[2]


def tensor_partners():
    t = lax.axis_index("tensor")
    pair, side = t // 2, lax.rem(t, 2)
    near = t + 1 - 2 * side
    cross = t + 2 - 4 * pair
    return pair, side, near, cross, 3 - t


def tensor_sum_kernel(chunks, source, extra, result, extra_all, came, half_sum, crossed, *sems):
    send_sem, recv_sem, extra_send, extra_recv = sems
    dp, t = lax.axis_index("dp"), lax.axis_index("tensor")
    _, side, near, cross, last = tensor_partners()
    greet([(dp, near), (dp, cross), (dp, last)])
    half = source.shape[0] // 2
    piece = half // chunks

    def lines(which, j):
        return pl.ds(pl.multiple_of(which * half + j * piece, piece), piece)

    def copy(stage, j, source_ref, target_ref, device):
        return pltpu.make_async_remote_copy(
            src_ref=source_ref,
            dst_ref=target_ref,
            send_sem=send_sem.at[stage, j],
            recv_sem=recv_sem.at[stage, j],
            device_id=(dp, device),
            device_id_type=MESH,
        )

    def near_copy(j):
        return copy(0, j, source.at[lines(1 - side, j)], came.at[j], near)

    def cross_copy(j):
        return copy(1, j, half_sum.at[j], crossed.at[j], cross)

    def last_copy(j, which):
        return copy(2, j, result.at[lines(which, j)], result.at[lines(which, j)], near)

    def extra_copy(place, device):
        return pltpu.make_async_remote_copy(
            src_ref=extra,
            dst_ref=extra_all.at[t],
            send_sem=extra_send.at[place],
            recv_sem=extra_recv.at[place],
            device_id=(dp, device),
            device_id_type=MESH,
        )

    for j in range(chunks):
        near_copy(j).start()
    for place, device in enumerate((near, cross, last)):
        extra_copy(place, device).start()
    extra_all[t] = extra[...]
    add = lambda a, b: (a[...].astype(jnp.float32) + b[...].astype(jnp.float32)).astype(
        jnp.bfloat16
    )
    for j in range(chunks):
        near_copy(j).wait_recv()
        half_sum[j] = add(source.at[lines(side, j)], came.at[j])
        cross_copy(j).start()
    for j in range(chunks):
        cross_copy(j).wait_recv()
        result[lines(side, j), :] = add(half_sum.at[j], crossed.at[j])
        last_copy(j, side).start()
    for j in range(chunks):
        last_copy(j, 1 - side).wait_recv()
    for place, device in enumerate((near, cross, last)):
        extra_copy(place, device).wait()
    for j in range(chunks):
        near_copy(j).wait_send()
        cross_copy(j).wait_send()
        last_copy(j, side).wait_send()


def tensor_sum(source, extra, number, chunks):
    rows, columns = source.shape
    block = pltpu.VMEM((chunks, rows // 2 // chunks, columns), jnp.bfloat16)
    vmem = pl.BlockSpec(memory_space=pltpu.VMEM)
    sem = pltpu.SemaphoreType.DMA
    return pl.pallas_call(
        functools.partial(tensor_sum_kernel, chunks),
        out_shape=[
            jax.ShapeDtypeStruct(source.shape, jnp.bfloat16),
            jax.ShapeDtypeStruct((4, *extra.shape), jnp.float32),
        ],
        in_specs=[vmem] * 2,
        out_specs=[vmem] * 2,
        scratch_shapes=[
            block,
            block,
            block,
            sem((3, chunks)),
            sem((3, chunks)),
            sem((3,)),
            sem((3,)),
        ],
        compiler_params=pltpu.CompilerParams(
            collective_id=number, has_side_effects=True, vmem_limit_bytes=60 << 20
        ),
        name="tensor_sum",
    )(source, extra)


def tensor_share_kernel(chunks, source, result, came, pair_sum, crossed, *sems):
    send_sem, recv_sem = sems
    dp = lax.axis_index("dp")
    pair, side, near, cross, last = tensor_partners()
    greet([(dp, near), (dp, cross)])
    rows, width = result.shape
    piece = rows // chunks

    def part(j, owner):
        return (
            pl.ds(j * piece, piece),
            pl.ds(pl.multiple_of(owner * width, width), width),
        )

    def copy(stage, j, source_ref, target_ref, device):
        return pltpu.make_async_remote_copy(
            src_ref=source_ref,
            dst_ref=target_ref,
            send_sem=send_sem.at[stage, j],
            recv_sem=recv_sem.at[stage, j],
            device_id=(dp, device),
            device_id_type=MESH,
        )

    def near_copy(j, where):
        owner = near if where else last
        return copy(where, j, source.at[part(j, owner)], came.at[where, j], near)

    def cross_copy(j):
        return copy(2, j, pair_sum.at[j], crossed.at[j], cross)

    for j in range(chunks):
        for where in (0, 1):
            near_copy(j, where).start()
    f32 = jnp.float32
    for j in range(chunks):
        near_copy(j, 0).wait_recv()
        pair_sum[j] = (source[part(j, cross)].astype(f32) + came[0, j].astype(f32)).astype(
            jnp.bfloat16
        )
        cross_copy(j).start()
    t = lax.axis_index("tensor")
    for j in range(chunks):
        near_copy(j, 1).wait_recv()
        cross_copy(j).wait_recv()
        total = source[part(j, t)].astype(f32) + came[1, j].astype(f32)
        result[pl.ds(j * piece, piece), :] = (total + crossed[j].astype(f32)).astype(jnp.bfloat16)
    for j in range(chunks):
        near_copy(j, 0).wait_send()
        near_copy(j, 1).wait_send()
        cross_copy(j).wait_send()


def tensor_share(source, number, chunks):
    rows, columns = source.shape
    width = columns // 4
    piece = rows // chunks
    vmem = pl.BlockSpec(memory_space=pltpu.VMEM)
    sem = pltpu.SemaphoreType.DMA
    return pl.pallas_call(
        functools.partial(tensor_share_kernel, chunks),
        out_shape=jax.ShapeDtypeStruct((rows, width), jnp.bfloat16),
        in_specs=[vmem],
        out_specs=vmem,
        scratch_shapes=[
            pltpu.VMEM((2, chunks, piece, width), jnp.bfloat16),
            pltpu.VMEM((chunks, piece, width), jnp.bfloat16),
            pltpu.VMEM((chunks, piece, width), jnp.bfloat16),
            sem((3, chunks)),
            sem((3, chunks)),
        ],
        compiler_params=pltpu.CompilerParams(
            collective_id=number, has_side_effects=True, vmem_limit_bytes=60 << 20
        ),
        name="tensor_share",
    )(source)


def experts_kernel(
    x,
    branch,
    gain,
    router,
    ids,
    cot,
    w_in,
    w_out,
    slots,
    row_grad,
    mixed,
    dots,
    grad_in,
    grad_out,
    normed,
    rows,
    cot_rows,
    part_grad,
):
    tokens, width = x.shape
    hidden_units = w_out.shape[1]
    f32, low = jnp.float32, jnp.bfloat16
    tile = 512

    @pl.loop(0, tokens // 64)
    def _(turn):
        here = pl.ds(pl.multiple_of(turn * 64, 64), 64)
        hidden = x[here, :].astype(f32) + branch[here, :].astype(f32)
        scale = lax.rsqrt(jnp.mean(hidden * hidden, axis=-1, keepdims=True) + EPSILON)
        normed[here, :] = (hidden * scale * gain[...]).astype(low)

    before = (
        lax.broadcasted_iota(jnp.int32, (tokens, tokens), 0)
        <= lax.broadcasted_iota(jnp.int32, (tokens, tokens), 1)
    ).astype(low)

    @pl.loop(0, w_in.shape[0])
    def _(e):
        chosen = jnp.max((ids[...] == e).astype(f32), axis=0, keepdims=True)
        rank = jnp.dot(
            jnp.broadcast_to(chosen, (8, tokens)).astype(low), before, preferred_element_type=f32
        )[0:1]
        slot = lax.broadcasted_iota(jnp.int32, (CAP, tokens), 0).astype(f32) + 1.0
        picked = jnp.where((rank == slot) & (chosen > 0.0), 1.0, 0.0)
        live = jnp.sum(picked, axis=1, keepdims=True)
        picked = picked.astype(low)
        slots[e] = picked

        @pl.loop(0, width // tile)
        def _(j):
            here = pl.ds(pl.multiple_of(j * tile, tile), tile)
            rows[:, here] = jnp.dot(picked, normed[:, here], preferred_element_type=f32).astype(low)
            cot_rows[:, here] = jnp.dot(picked, cot[:, here], preferred_element_type=f32).astype(
                low
            )

        logits = across_rows(rows[...], router[...])
        shifted = jnp.exp(logits - jnp.max(logits, axis=-1, keepdims=True))
        expert = lax.broadcasted_iota(jnp.int32, logits.shape, 1)
        gate = (
            jnp.sum(jnp.where(expert == e, shifted, 0.0), axis=-1, keepdims=True)
            / jnp.sum(shifted, axis=-1, keepdims=True)
            * live
        )
        into = jnp.dot(rows[...], w_in[e, 0], preferred_element_type=f32)
        up = jnp.dot(rows[...], w_in[e, 1], preferred_element_type=f32)
        sig = 1.0 / (1.0 + jnp.exp(-into))
        silu = into * sig
        active = (silu * up).astype(low)

        def forward(j, state):
            dot_sum, act_grad = state
            here = pl.ds(pl.multiple_of(j * tile, tile), tile)
            out = jnp.dot(active, w_out[e, :, here], preferred_element_type=f32)
            mixed[e, :, here] = (gate * out).astype(low)
            wide = cot_rows[:, here].astype(f32)
            grad = (gate * wide).astype(low)
            part_grad[:, here] = grad
            return (
                dot_sum + jnp.sum(wide * out, axis=-1, keepdims=True),
                act_grad + across_rows(grad, w_out[e, :, here]),
            )

        dot_sum, act_grad = lax.fori_loop(
            0,
            width // tile,
            forward,
            (jnp.zeros((CAP, 1), f32), jnp.zeros((CAP, hidden_units), f32)),
        )
        dots[e] = jnp.broadcast_to(dot_sum * live, (CAP, 128)).T[0:8]
        into_grad = (act_grad * up * (sig * (1.0 + into * (1.0 - sig)))).astype(low)
        up_grad = (act_grad * silu).astype(low)
        active_turned = active.astype(f32).T.astype(low)

        @pl.loop(0, width // tile)
        def _(j):
            here = pl.ds(pl.multiple_of(j * tile, tile), tile)
            row_grad[e, :, here] = (
                across_rows(into_grad, w_in[e, 0, here, :])
                + across_rows(up_grad, w_in[e, 1, here, :])
            ).astype(low)
            grad_out[e, :, here] = jnp.dot(
                active_turned, part_grad[:, here], preferred_element_type=f32
            ).astype(low)
            turned = rows[:, here].astype(f32).T.astype(low)
            grad_in[e, here, 0:hidden_units] = jnp.dot(
                turned, into_grad, preferred_element_type=f32
            ).astype(low)
            grad_in[e, here, hidden_units:] = jnp.dot(
                turned, up_grad, preferred_element_type=f32
            ).astype(low)


def experts_call(x, branch, gain, router, ids, cot, w_in, w_out):
    tokens, width = x.shape
    window, hidden_units = w_out.shape[:2]
    shape, low = jax.ShapeDtypeStruct, jnp.bfloat16
    vmem = pl.BlockSpec(memory_space=pltpu.VMEM)
    return pl.pallas_call(
        experts_kernel,
        out_shape=[
            shape((window, CAP, tokens), low),
            shape((window, CAP, width), low),
            shape((window, CAP, width), low),
            shape((window, 8, CAP), jnp.float32),
            shape((window, width, 2 * hidden_units), low),
            shape((window, hidden_units, width), low),
        ],
        in_specs=[vmem] * 8,
        out_specs=[vmem] * 6,
        scratch_shapes=[
            pltpu.VMEM((tokens, width), low),
            pltpu.VMEM((CAP, width), low),
            pltpu.VMEM((CAP, width), low),
            pltpu.VMEM((CAP, width), low),
        ],
        compiler_params=pltpu.CompilerParams(vmem_limit_bytes=60 << 20),
        name="experts",
    )(x, branch, gain, router, ids, cot, w_in, w_out)


def row_scale(values):
    return lax.rsqrt(jnp.mean(values * values, axis=-1, keepdims=True) + EPSILON)


def rotate(values, positions):
    half_dim = values.shape[-1] // 2
    inv_freq = ROPE_BASE ** (-(jnp.arange(half_dim, dtype=jnp.float32) * 2.0) / values.shape[-1])
    turn_angle = positions.astype(jnp.float32)[:, None] * inv_freq[None, :]
    cosine = jnp.cos(turn_angle)[:, None, :]
    sine_vals = jnp.sin(turn_angle)[:, None, :]
    first_half = values[..., :half_dim]
    second_half = values[..., half_dim:]
    return jnp.concatenate(
        [
            first_half * cosine - second_half * sine_vals,
            second_half * cosine + first_half * sine_vals,
        ],
        axis=-1,
    )


def token_tables(seq_blocks, block_place, row_ids):
    block_total = block_place.shape[0]
    seq_total = seq_blocks.shape[0]
    seq_ends = jnp.cumsum(seq_blocks)
    seq_firsts = seq_ends - seq_blocks
    given_block = row_ids // BLOCK
    packed = jnp.sum(
        jnp.where(
            given_block[:, None] == jnp.arange(block_total, dtype=jnp.int32)[None, :],
            block_place[None, :],
            0,
        ),
        axis=1,
    )
    seq_of = jnp.sum((packed[:, None] >= seq_ends[None, :]).astype(jnp.int32), axis=1)
    first_of = jnp.sum(
        jnp.where(
            seq_of[:, None] == jnp.arange(seq_total, dtype=jnp.int32)[None, :],
            seq_firsts[None, :],
            0,
        ),
        axis=1,
    )
    return (seq_of, (packed - first_of) * BLOCK + row_ids % BLOCK)


def norm_back(values, row_factor, gain_row, incoming, model_width):
    scaled = gain_row * incoming
    inner_sum = jnp.sum(scaled * values, axis=-1, keepdims=True)
    return row_factor * scaled - values * (row_factor**3 / model_width) * inner_sum


def body(
    tokens,
    seq_blocks,
    block_place,
    pad_mask,
    expert_ids,
    attn_gain,
    w_qkv,
    qk_gain,
    w_out,
    ffn_gain,
    router,
    expert_in,
    expert_out,
    cotangent,
):
    rows_here = tokens.shape[0]
    model_width = tokens.shape[1]
    local_width = w_qkv.shape[2]
    heads_here = local_width // HDIM
    local_ff = expert_out.shape[1]
    tensor_index = lax.axis_index("tensor")
    feature_start = tensor_index * local_width
    first_row = lax.axis_index("dp") * rows_here
    row_ids = first_row + jnp.arange(rows_here, dtype=jnp.int32)
    seg_q, pos_q = token_tables(seq_blocks, block_place, row_ids)
    inputs = tokens.astype(jnp.float32)
    x_scale = row_scale(inputs)
    normed_in = (inputs * x_scale * attn_gain).astype(jnp.bfloat16)
    projected = jnp.dot(
        normed_in, w_qkv.reshape(model_width, 3 * local_width), preferred_element_type=jnp.float32
    ).reshape(rows_here, 3, local_width)
    queries = projected[:, 0]
    keys_here = projected[:, 1]
    values_here = projected[:, 2]
    sums_q, sums_k = lax.psum(
        (jnp.sum(queries * queries, axis=-1), jnp.sum(keys_here * keys_here, axis=-1)), "tensor"
    )
    q_scale = lax.rsqrt(sums_q / model_width + EPSILON)[:, None]
    k_scale = lax.rsqrt(sums_k / model_width + EPSILON)[:, None]
    q_norm = (queries * q_scale * qk_gain[0]).reshape(rows_here, heads_here, HDIM)
    k_norm = (keys_here * k_scale * qk_gain[1]).reshape(rows_here, heads_here, HDIM)
    q_rot = rotate(q_norm, pos_q).astype(jnp.bfloat16)
    k_rot = rotate(k_norm, pos_q).astype(jnp.bfloat16)
    v_low = values_here.astype(jnp.bfloat16)
    keep_here = pad_mask.astype(jnp.bfloat16)
    dp_count = lax.axis_size("dp")
    q_line, k_all, v_all, keep_all, cot_low, w_split = spread_heads(
        q_rot.reshape(rows_here, local_width),
        k_rot.reshape(rows_here, local_width),
        v_low,
        jnp.broadcast_to(keep_here[None], (8, rows_here)),
        cotangent,
        expert_in,
        dp_count,
        heads_here,
        1,
    )
    tables = block_tables(
        seq_blocks, block_place, keep_all[:, 0], rows_here, heads_here, dp_count
    )
    total_rows = dp_count * rows_here
    line_out, attend_back = attend_calls(
        tables,
        q_line.reshape(heads_here * rows_here, HDIM),
        k_all.reshape(total_rows, HDIM),
        v_all.reshape(total_rows, HDIM),
    )
    attended_low = swap_line(
        line_out.reshape(heads_here, rows_here, HDIM), dp_count, heads_here, True, 2
    )
    branch_low, _ = tensor_sum(
        jnp.dot(attended_low, w_out, preferred_element_type=jnp.float32).astype(jnp.bfloat16),
        jnp.zeros((8, 128), jnp.float32),
        5,
        4,
    )
    slots, slot_grad, slot_mixed, slot_dots, expert_in_grad, expert_out_grad = experts_call(
        tokens,
        branch_low,
        ffn_gain[None],
        jnp.transpose(router),
        jnp.transpose(expert_ids),
        cot_low,
        w_split,
        expert_out,
    )
    slot_grad, dots_all = tensor_sum(
        slot_grad.reshape(WIN * CAP, model_width), slot_dots.reshape(WIN * 8, CAP), 6, 2
    )
    flat_slots = slots.reshape(WIN * CAP, rows_here)
    mixture_grad = jnp.einsum("ct,cd->td", flat_slots, slot_grad, preferred_element_type=jnp.float32)
    slot_dots = jnp.sum(dots_all, axis=0).reshape(WIN, 8, CAP)[:, 0]
    gate_grad = jnp.transpose(
        jnp.sum(jnp.where(slots > 0, slot_dots[:, :, None], 0.0), axis=1)
    )
    hidden = inputs + branch_low.astype(jnp.float32)
    h_scale = row_scale(hidden)
    normed = (hidden * h_scale * ffn_gain).astype(jnp.bfloat16)
    logits = jnp.dot(normed, router, preferred_element_type=jnp.float32)
    router_probs = jax.nn.softmax(logits, axis=-1)
    hidden_share = lax.dynamic_slice_in_dim(hidden, feature_start, local_width, 1)
    cot_full = cot_low.astype(jnp.float32)
    probs_grad = jnp.concatenate(
        [gate_grad, jnp.zeros((rows_here, router.shape[1] - WIN), jnp.float32)],
        axis=1,
    )
    logit_grad = (
        router_probs * (probs_grad - jnp.sum(router_probs * probs_grad, axis=-1, keepdims=True))
    ).astype(jnp.bfloat16)
    normed_grad = mixture_grad + jnp.einsum(
        "te,de->td", logit_grad, router, preferred_element_type=jnp.float32
    )
    normed_share = lax.dynamic_slice_in_dim(normed, feature_start, local_width, 1)
    router_grad = jnp.einsum(
        "td,te->de", normed_share, logit_grad, preferred_element_type=jnp.float32
    )
    ffn_gain_grad = lax.dynamic_slice_in_dim(
        jnp.sum(normed_grad * hidden * h_scale, axis=0), feature_start, local_width, 0
    )
    hidden_grad = cot_full + norm_back(hidden, h_scale, ffn_gain, normed_grad, model_width)
    branch_grad = hidden_grad.astype(jnp.bfloat16)
    out_grad = jnp.einsum(
        "tc,td->cd", attended_low, branch_grad, preferred_element_type=jnp.float32
    )
    attended_grad = jnp.einsum(
        "td,cd->tc", branch_grad, w_out, preferred_element_type=jnp.float32
    ).astype(jnp.bfloat16)
    line_grad = swap_line(attended_grad, dp_count, heads_here, False, 3)
    dq_line, dk_line, dv_line = attend_back(line_grad.reshape(heads_here * rows_here, HDIM))
    query_grad, key_grad, value_low_grad = return_heads(
        dq_line.reshape(heads_here, rows_here, HDIM),
        dk_line.reshape(dp_count, rows_here, HDIM),
        dv_line.reshape(dp_count, rows_here, HDIM),
        dp_count,
        heads_here,
        4,
    )
    query_grad = query_grad.astype(jnp.float32).reshape(rows_here, heads_here, HDIM)
    key_grad = key_grad.astype(jnp.float32)
    _, rope_pull = jax.vjp(lambda turned: rotate(turned, pos_q), q_norm)
    q_norm_grad = rope_pull(query_grad)[0].reshape(rows_here, local_width)
    k_norm_grad = rope_pull(key_grad.reshape(rows_here, heads_here, HDIM))[0].reshape(
        rows_here, local_width
    )
    scaled_q = qk_gain[0] * q_norm_grad
    scaled_k = qk_gain[1] * k_norm_grad
    inner_q, inner_k = lax.psum(
        (jnp.sum(scaled_q * queries, axis=-1), jnp.sum(scaled_k * keys_here, axis=-1)), "tensor"
    )
    q_grad = (
        q_scale * scaled_q - queries * (q_scale**3 / model_width) * inner_q[:, None]
    ).astype(jnp.bfloat16)
    k_grad = (
        k_scale * scaled_k - keys_here * (k_scale**3 / model_width) * inner_k[:, None]
    ).astype(jnp.bfloat16)
    qk_gain_grad = jnp.stack(
        [
            jnp.sum(q_norm_grad * queries * q_scale, axis=0),
            jnp.sum(k_norm_grad * keys_here * k_scale, axis=0),
        ]
    )
    proj_grad = jnp.stack([q_grad, k_grad, value_low_grad], axis=1).reshape(
        rows_here, 3 * local_width
    )
    qkv_grad = jnp.einsum(
        "td,tc->dc", normed_in, proj_grad, preferred_element_type=jnp.float32
    ).reshape(model_width, 3, local_width)
    normed_in_grad = jnp.einsum(
        "tc,dc->td",
        proj_grad,
        w_qkv.reshape(model_width, 3 * local_width),
        preferred_element_type=jnp.float32,
    )
    input_part = norm_back(inputs, x_scale, attn_gain, normed_in_grad, model_width)
    gain_part = jnp.sum(normed_in_grad * inputs * x_scale, axis=0)
    shares = tensor_share(
        jnp.concatenate(
            [
                input_part.astype(jnp.bfloat16),
                slot_mixed.reshape(WIN * CAP, model_width),
                jnp.broadcast_to(gain_part.astype(jnp.bfloat16)[None], (32, model_width)),
            ]
        ),
        7,
        2,
    )
    input_sum = shares[:rows_here].astype(jnp.float32)
    mixture_share = jnp.einsum(
        "ct,cd->td",
        flat_slots,
        shares[rows_here : rows_here + WIN * CAP],
        preferred_element_type=jnp.float32,
    )
    output = (hidden_share + mixture_share).astype(jnp.bfloat16)
    attn_gain_grad = shares[rows_here + WIN * CAP].astype(jnp.float32)
    input_grad = (
        lax.dynamic_slice_in_dim(hidden_grad, feature_start, local_width, 1) + input_sum
    ).astype(jnp.bfloat16)
    small = jnp.concatenate(
        [
            router_grad.reshape(-1, 256),
            jnp.concatenate([attn_gain_grad, ffn_gain_grad, qk_gain_grad.reshape(-1)]).reshape(
                -1, 256
            ),
        ]
    ).astype(jnp.bfloat16)
    small_rows = small.shape[0]
    small = jnp.pad(small, ((0, -small_rows % (dp_count * 8)), (0, 0)))
    low = jnp.bfloat16
    qkv_sum, out_sum, in_sum, exp_sum, small_sum = ring_sum(
        [
            jnp.transpose(qkv_grad, (1, 0, 2)).astype(low),
            out_grad.astype(low)[None],
            expert_in_grad,
            expert_out_grad,
            small[None],
        ],
        dp_count,
        0,
    )
    qkv_grad = jnp.transpose(qkv_sum.astype(jnp.float32), (1, 0, 2))
    out_grad = out_sum[0].astype(jnp.float32)
    expert_in_grad = in_sum.astype(jnp.float32).reshape(expert_in.shape)
    expert_out_grad = exp_sum.astype(jnp.float32)
    router_rows = router_grad.size // 256
    small_sum = small_sum[0].astype(jnp.float32)
    router_grad = small_sum[:router_rows].reshape(router_grad.shape)
    gains = small_sum[router_rows:small_rows].reshape(-1)
    attn_gain_grad = gains[:local_width]
    ffn_gain_grad = gains[local_width : 2 * local_width]
    qk_gain_grad = gains[2 * local_width :].reshape(2, local_width)
    return (
        output,
        input_grad,
        attn_gain_grad,
        qkv_grad,
        qk_gain_grad,
        out_grad,
        ffn_gain_grad,
        router_grad,
        expert_in_grad,
        expert_out_grad,
    )


def solution(mesh):
    placed = (
        P("dp", None),
        P(),
        P(),
        P("dp"),
        P("dp", None),
        P(),
        P(None, None, "tensor"),
        P(None, "tensor"),
        P("tensor", None),
        P(),
        P(),
        P(None, None, None, "tensor"),
        P(None, "tensor", None),
        P("dp", "tensor"),
    )
    return jax.shard_map(
        body,
        mesh=mesh,
        in_specs=placed,
        out_specs=(
            P("dp", "tensor"),
            P("dp", "tensor"),
            P("tensor"),
            P(None, None, "tensor"),
            P(None, "tensor"),
            P("tensor", None),
            P("tensor"),
            P("tensor", None),
            P(None, None, None, "tensor"),
            P(None, "tensor", None),
        ),
        check_vma=False,
    )
```
